256 devices in a mesh: lon: 32 (over y_hi, z, core), lat: 8 (over x, y_lo).
Axes of the slice: x: 4, y: 4 (y_hi: 2, y_lo: 2; y = y_hi * 2 + y_lo), z: 8, core: 2. Of those that a mesh axis runs over, the one named last changes fastest.
Arguments:
- inputs: bfloat16 [256, 1024, 192], P('lat', 'lon'), may hold values from -6 to 6
- cotangent: bfloat16 [256, 1024, 192], P('lat', 'lon'), may hold values from -6 to 6
- first_weight: bfloat16 [3, 3, 192, 192], replicated, may hold values from -0.15625 to 0.15625
- second_weight: bfloat16 [3, 3, 192, 192], replicated, may hold values from -0.15625 to 0.15625
Outputs:
- input_gradient: bfloat16 [256, 1024, 192], P('lat', 'lon')
- first_kernel_gradient: float32 [3, 3, 192, 192], replicated
- second_kernel_gradient: float32 [3, 3, 192, 192], replicated
The draws below stay inside these ranges and needn't reach their ends.
All inputs are finite; a program needn't handle non-finite values.
Results may differ from the reference program's by a relative error of at most 0.0049.
Values may be sent and summed in bfloat16 or wider, within the bound.
A program may use at most 128 MiB of HBM per device.

```python
import math
import jax
import jax.numpy as jnp

C = 192
FIRST_SPREAD = 32
SECOND_SPREAD = 64
LAT = 256
LON = 1024


def block_scale(own_key, dims, pieces, least, high):
    factor_of = 1.0
    for dim, shards_of in pieces:
        draws = jax.random.uniform(jax.random.fold_in(jax.random.fold_in(own_key, 6), dim), (shards_of,), jnp.float32, least / len(pieces), high / len(pieces))
        factor_of = factor_of * jnp.repeat(jnp.exp(draws), dims[dim] // shards_of).reshape((-1,) + (1,) * (len(dims) - 1 - dim))
    return factor_of


def noise(stream_key, shape, deviation, reach, shards=(), dtype=jnp.bfloat16):
    values = deviation * jax.random.normal(stream_key, shape, jnp.float32)
    if shards:
        values = values * block_scale(stream_key, shape, shards, -0.22, 0.18)
    return jnp.clip(values, -reach, reach).astype(dtype)


def setup_inputs(seed: int = 0) -> dict:
    streams_of = jax.random.split(jax.random.key(seed), 5)
    inputs = noise(streams_of[0], (LAT, LON, C), 1.0, 6.0, ((0, 8), (1, 32)))
    cotangent = noise(streams_of[1], (LAT, LON, C), 1.0, 6.0, ((0, 8), (1, 32)))
    first_weight = noise(streams_of[2], (3, 3, C, C), (9 * C) ** -0.5, 0.15625)
    second_weight = noise(streams_of[3], (3, 3, C, C), (9 * C) ** -0.5, 0.15625)
    return dict(inputs=inputs, cotangent=cotangent, first_weight=first_weight, second_weight=second_weight)


def shifted_taps(field, dilation):
    padded = jnp.pad(field, ((1, 1), (0, 0), (0, 0)))
    height = field.shape[0]
    result = []
    for row_off in (-1, 0, 1):
        band = padded[1 + row_off:1 + row_off + height]
        for col_off in (-1, 0, 1):
            result.append(jnp.roll(band, -col_off * dilation, axis=1))
    return result

def apply_convolution(field, weight, dilation):
    channels = field.shape[2]
    shape = (field.shape[0], field.shape[1], weight.shape[3])
    total = jnp.zeros(shape, jnp.float32)
    for index, tapped in enumerate(shifted_taps(field, dilation)):
        product = jnp.dot(tapped.reshape(-1, channels), weight[index // 3, index % 3], preferred_element_type=jnp.float32)
        total = total + product.reshape(shape)
    return total

def cross_correlate(field, other, dilation):
    channels = field.shape[2]
    flat_other = other.reshape(-1, channels)
    blocks = []
    for tapped in shifted_taps(field, dilation):
        blocks.append(jnp.dot(tapped.reshape(-1, channels).T, flat_other, preferred_element_type=jnp.float32))
    return jnp.stack(blocks).reshape(3, 3, channels, channels)

def flipped_kernel(weight):
    return jnp.transpose(weight[::-1, ::-1], (0, 1, 3, 2))

def reference(inputs, cotangent, first_weight, second_weight):
    gradient_scale = 1.0 / math.sqrt(LAT * LON)
    pre_activation = apply_convolution(inputs, first_weight, FIRST_SPREAD)
    hidden_state = jax.nn.silu(pre_activation).astype(jnp.bfloat16)
    hidden_gradient = apply_convolution(cotangent, flipped_kernel(second_weight), SECOND_SPREAD)
    second_kernel_gradient = cross_correlate(hidden_state, cotangent, SECOND_SPREAD) * gradient_scale
    sigma = jax.nn.sigmoid(pre_activation)
    pre_activation_gradient = (hidden_gradient * sigma * (1.0 + pre_activation * (1.0 - sigma))).astype(jnp.bfloat16)
    input_gradient = apply_convolution(pre_activation_gradient, flipped_kernel(first_weight), FIRST_SPREAD).astype(jnp.bfloat16)
    first_kernel_gradient = cross_correlate(inputs, pre_activation_gradient, FIRST_SPREAD) * gradient_scale
    return (input_gradient, first_kernel_gradient, second_kernel_gradient)
```

```python
import functools
import math

import jax
import jax.numpy as jnp
from jax import lax
from jax.experimental import pallas as pl
from jax.experimental.pallas import tpu as pltpu
from jax.sharding import PartitionSpec as P

MESH = pl.DeviceIdType.MESH
BF = jnp.bfloat16
F32 = jnp.float32
ROW = 32
CELLS = 1024
EXT = 1152
C = 192
CP = 256
BLK = 256
UNITS = 336
TAPU = 36


def pack(cells):
    half = cells.shape[0] // 2
    tail = jnp.concatenate([cells[:half, 128:C], cells[half:, 128:C]], axis=1)
    return cells[:, :128], tail


def unpack_into(ref, slot, start, packed):
    n = packed.shape[0] * 2 // 3
    tail = packed[n:]
    zero = jnp.zeros((n // 2, 64), packed.dtype)
    ref[slot, start:start + n, 0:128] = packed[:n]
    ref[slot, start:start + n // 2, 128:256] = jnp.concatenate([tail[:, :64], zero], axis=1)
    ref[slot, start + n // 2:start + n, 128:256] = jnp.concatenate([tail[:, 64:], zero], axis=1)


class Exchange:
    def __init__(self, bufs, dist, lon, lat, n_lon, n_lat):
        (self.slab, self.rows, self.slab_in, self.rows_in,
         self.send, self.recv, self.ext) = bufs
        self.lat, self.n_lat = lat, n_lat
        self.behind = lax.rem(lon + dist, n_lon)
        self.ahead = lax.rem(lon + n_lon - dist, n_lon)
        self.lon = lon

    def targets(self):
        return (self.behind, self.ahead, self.lon)

    def slab_copy(self, k):
        return pltpu.make_async_remote_copy(
            src_ref=self.slab, dst_ref=self.slab_in.at[k],
            send_sem=self.send.at[k], recv_sem=self.recv.at[k],
            device_id={"lon": self.targets()[k], "lat": self.lat}, device_id_type=MESH)

    def row_copy(self, k, side):
        s = 2 + 2 * k + side
        lat = jnp.minimum(self.lat + 1, self.n_lat - 1) if side == 0 else jnp.maximum(self.lat - 1, 0)
        return pltpu.make_async_remote_copy(
            src_ref=self.rows.at[side], dst_ref=self.rows_in.at[2 * k + side],
            send_sem=self.send.at[s], recv_sem=self.recv.at[s],
            device_id={"lon": self.targets()[k], "lat": lat}, device_id_type=MESH)

    def load(self, cells):
        main, tail = pack(cells)
        self.slab[0:CELLS] = main
        self.slab[CELLS:] = tail
        for side, part in ((0, cells[CELLS - ROW:]), (1, cells[:ROW])):
            main, tail = pack(part)
            self.rows[side, 0:ROW] = main
            self.rows[side, ROW:] = tail

    def start(self):
        for k in (0, 1):
            self.slab_copy(k).start()

    def start_rows(self):
        for k in range(3):
            @pl.when(self.lat < self.n_lat - 1)
            def _():
                self.row_copy(k, 0).start()

            @pl.when(self.lat > 0)
            def _():
                self.row_copy(k, 1).start()

    def place_own(self, cells):
        self.ext[1, ROW:ROW + CELLS, 0:128] = cells[:, :128]
        self.ext[1, ROW:ROW + CELLS, 128:256] = jnp.concatenate(
            [cells[:, 128:C], jnp.zeros((CELLS, 64), BF)], axis=1)

    def arrive_rows(self, k):
        slot = (0, 2, 1)[k]
        zero = jnp.zeros((ROW, CP), BF)
        for side, start, here in ((0, 0, self.lat > 0), (1, ROW + CELLS, self.lat < self.n_lat - 1)):
            @pl.when(here)
            def _():
                self.row_copy(k, side).wait_recv()
                unpack_into(self.ext, slot, start, self.rows_in[2 * k + side])

            @pl.when(jnp.logical_not(here))
            def _():
                self.ext[slot, start:start + ROW] = zero
        self.ext[slot, ROW * 2 + CELLS:] = jnp.zeros((EXT - 2 * ROW - CELLS, CP), BF)

    def arrive(self, k):
        slot = (0, 2)[k]
        self.slab_copy(k).wait_recv()
        unpack_into(self.ext, slot, ROW, self.slab_in[k])

    def drain(self):
        for k in (0, 1):
            self.slab_copy(k).wait_send()
        for k in range(3):
            @pl.when(self.lat < self.n_lat - 1)
            def _():
                self.row_copy(k, 0).wait_send()

            @pl.when(self.lat > 0)
            def _():
                self.row_copy(k, 1).wait_send()


def exchange_scratch():
    return [
        pltpu.VMEM((CELLS * 3 // 2, 128), BF),
        pltpu.VMEM((2, ROW * 3 // 2, 128), BF),
        pltpu.VMEM((2, CELLS * 3 // 2, 128), BF),
        pltpu.VMEM((6, ROW * 3 // 2, 128), BF),
        pltpu.SemaphoreType.DMA((8,)),
        pltpu.SemaphoreType.DMA((8,)),
        pltpu.VMEM((3, EXT, CP), BF),
    ]


def kernel(n_lon, n_lat, x_ref, c_ref, w1_ref, w2_ref, dx_ref, ff_ref, *scratch):
    xb, cb, pb = scratch[0:7], scratch[7:14], scratch[14:21]
    (w1n, w1t, w2t, acc_x, acc_c, hid_t, x_t, gz,
     part, pair_in, s0, r1, s1, r2, r3, pair_sem, ssem1, rsem1, ssem2, rsem2,
     ssem3, rsem3, ssem4, rsem4, ssem5, rsem5, pair_sem2, ff) = scratch[21:]
    lon, lat = lax.axis_index("lon"), lax.axis_index("lat")
    core = lax.rem(lon, 2)
    z = lax.rem(lon // 2, 8)
    y = (lon // 16) * 2 + lax.rem(lat, 2)
    x = lat // 2

    def at(xx, yy, zz):
        return {"lon": (yy // 2) * 16 + zz * 2 + core, "lat": xx * 2 + lax.rem(yy, 2)}

    def first(k):
        return at(lax.rem(x + k * (1 - core), 4), lax.rem(y + k * core, 4), z)

    def second(k):
        return at(lax.rem(x + k * core, 4), lax.rem(y + k * (1 - core), 4), z)

    def third(k):
        return at(x, y, lax.rem(z + k, 8))

    partner = {"lon": lon + 1 - 2 * core, "lat": lat}
    pos1 = x * (1 - core) + y * core
    pos2 = y * (1 - core) + x * core

    barrier = pltpu.get_barrier_semaphore()

    def greet(dev):
        pl.semaphore_signal(barrier, inc=1, device_id=dev, device_id_type=MESH)

    for dl in (-2, -1, 1, 2):
        greet({"lon": lax.rem(lon + n_lon + dl, n_lon), "lat": lat})
    for da, here in ((-1, lat > 0), (1, lat < n_lat - 1)):
        @pl.when(here)
        def _():
            for dl in (-2, -1, 0, 1, 2):
                greet({"lon": lax.rem(lon + n_lon + dl, n_lon), "lat": lat + da})
    for k in (1, 2, 3):
        greet(first(k))
        greet(second(k))
    for k in range(1, 8):
        greet(third(k))

    xe = Exchange(xb, 1, lon, lat, n_lon, n_lat)
    ce = Exchange(cb, 2, lon, lat, n_lon, n_lat)
    pe = Exchange(pb, 1, lon, lat, n_lon, n_lat)
    xcells, ccells = x_ref[...], c_ref[...]
    xe.load(xcells)
    ce.load(ccells)
    beside = jnp.where(lat > 0, 5, 0) + jnp.where(lat < n_lat - 1, 5, 0)
    pl.semaphore_wait(barrier, 4 + 6 + 7 + beside)
    xe.start()
    ce.start()
    xe.start_rows()
    ce.start_rows()

    w1n[...] = jnp.zeros_like(w1n)
    w1t[...] = jnp.zeros_like(w1t)
    w2t[...] = jnp.zeros_like(w2t)
    for b in range(3):
        for a in range(3):
            w1n[b, a * CP:a * CP + C, 0:C] = w1_ref[a * 3 + b]
            w1t[b, 0:C, a * CP:a * CP + C] = w1_ref[(2 - a) * 3 + 2 - b]
            w2t[b, 0:C, a * CP:a * CP + C] = w2_ref[(2 - a) * 3 + 2 - b]
    gz[0:2 * ROW] = jnp.zeros((2 * ROW, CP), BF)
    gz[2 * ROW + CELLS:] = jnp.zeros((gz.shape[0] - 2 * ROW - CELLS, CP), BF)
    xe.place_own(xcells)
    ce.place_own(ccells)

    def taps(ext, slot, i):
        start = pl.multiple_of(i * BLK, BLK)
        return jnp.concatenate([ext[slot, pl.ds(start + a * ROW, BLK), :] for a in range(3)], axis=1)

    def straight(ext, slot, i, w):
        return jnp.dot(taps(ext, slot, i), w[slot], preferred_element_type=F32)

    def flipped(ext, slot, i, w):
        return lax.dot_general(taps(ext, slot, i), w[slot], (((1,), (1,)), ((), ())),
                               preferred_element_type=F32)

    def rows_of(i):
        return pl.ds(pl.multiple_of(i * BLK, BLK), BLK)

    def add_slab(acc, conv, ext, slot, w, new):
        @pl.loop(0, CELLS // BLK)
        def _(i):
            value = conv(ext, slot, i, w)
            acc[rows_of(i)] = value if new else acc[rows_of(i)] + value

    def put_tap(which, tap, grad):
        main = grad[:, :128].reshape(24, 8, 128)
        tail = jnp.concatenate([grad[:96, 128:C], grad[96:, 128:C]], axis=1).reshape(12, 8, 128)
        part[which, pl.ds(tap * TAPU, 24)] = main.astype(BF)
        part[which, pl.ds(tap * TAPU + 24, 12)] = tail.astype(BF)

    xe.arrive_rows(2)
    add_slab(acc_x, straight, xe.ext, 1, w1n, True)
    ce.arrive_rows(2)
    add_slab(acc_c, flipped, ce.ext, 1, w2t, True)
    x_t[1] = xe.ext[1].T
    for k, slot in ((0, 0), (1, 2)):
        xe.arrive_rows(k)
        xe.arrive(k)
        add_slab(acc_x, straight, xe.ext, slot, w1n, False)
        x_t[slot] = xe.ext[slot].T

    @pl.loop(0, CELLS // BLK)
    def _(i):
        pre = acc_x[rows_of(i)]
        sig = 1.0 / (1.0 + jnp.exp(-pre))
        hid_t[:, rows_of(i)] = (pre * sig).astype(BF).T
        acc_x[rows_of(i)] = sig * (1.0 + pre * (1.0 - sig))

    def second_grad(slot):
        @pl.loop(0, 3)
        def _(a):
            rhs = ce.ext[slot, pl.ds(pl.multiple_of((2 - a) * ROW, ROW), CELLS), :]
            put_tap(1, a * 3 + 2 - slot, jnp.dot(hid_t[0:C], rhs, preferred_element_type=F32))

    second_grad(1)
    for k, slot in ((0, 0), (1, 2)):
        ce.arrive_rows(k)
        ce.arrive(k)
        add_slab(acc_c, flipped, ce.ext, slot, w2t, False)
        second_grad(slot)

    @pl.loop(0, CELLS // BLK)
    def _(i):
        gz[pl.ds(pl.multiple_of(i * BLK + 2 * ROW, 2 * ROW), BLK)] = (
            acc_c[rows_of(i)] * acc_x[rows_of(i)]).astype(BF)
    pcells = gz[2 * ROW:2 * ROW + CELLS]
    pe.load(pcells[:, :C])
    pe.start()
    pe.start_rows()

    @pl.loop(0, 3)
    def _(a):
        rhs = gz[pl.ds(pl.multiple_of((2 - a) * ROW, ROW), EXT), :]
        for b in range(3):
            put_tap(0, a * 3 + b, jnp.dot(x_t[b, 0:C], rhs, preferred_element_type=F32))
    part[0, 324:] = jnp.zeros((UNITS - 324, 8, 128), BF)
    part[1, 324:] = jnp.zeros((UNITS - 324, 8, 128), BF)

    def remote(src, dst, ss, rs, dev):
        return pltpu.make_async_remote_copy(src_ref=src, dst_ref=dst, send_sem=ss, recv_sem=rs,
                                            device_id=dev, device_id_type=MESH)

    swap = remote(part.at[1 - core], pair_in, pair_sem.at[0], pair_sem.at[1], partner)
    swap.start()
    pe.place_own(pcells[:, :C])
    pe.arrive_rows(2)
    add_slab(acc_x, flipped, pe.ext, 1, w1t, True)
    swap.wait()
    s0[...] = (part[core].astype(F32) + pair_in[...].astype(F32)).astype(BF)
    QUART, SIX = UNITS // 4, UNITS // 16

    def chunk(ref, pos, size):
        return ref.at[pl.ds(pos * size, size)]

    def one(k):
        return remote(chunk(s0, lax.rem(pos1 + k, 4), QUART), r1.at[k - 1],
                      ssem1.at[k - 1], rsem1.at[k - 1], first(k))

    def two(k):
        return remote(chunk(s1, lax.rem(pos2 + k, 4), SIX), r2.at[k - 1],
                      ssem2.at[k - 1], rsem2.at[k - 1], second(k))

    def three(k):
        return remote(r3.at[z], r3.at[z], ssem3.at[k - 1], rsem3.at[k - 1], third(k))

    def three_in(k):
        spot = r3.at[lax.rem(z + 8 - k, 8)]
        return remote(spot, spot, ssem3.at[k - 1], rsem3.at[k - 1], third(k))

    def own(pos, size):
        return ff.at[core, pl.ds(pos, size)]

    def four(k):
        spot = own(pos1 * QUART + pos2 * SIX, SIX)
        return remote(spot, spot, ssem4.at[k - 1], rsem4.at[k - 1], second(k))

    def four_in(k):
        spot = own(pos1 * QUART + lax.rem(pos2 + 4 - k, 4) * SIX, SIX)
        return remote(spot, spot, ssem4.at[k - 1], rsem4.at[k - 1], second(k))

    def five(k):
        spot = own(pos1 * QUART, QUART)
        return remote(spot, spot, ssem5.at[k - 1], rsem5.at[k - 1], first(k))

    def five_in(k):
        spot = own(lax.rem(pos1 + 4 - k, 4) * QUART, QUART)
        return remote(spot, spot, ssem5.at[k - 1], rsem5.at[k - 1], first(k))

    for k in (1, 2, 3):
        one(k).start()
    pe.arrive_rows(0)
    pe.arrive(0)
    add_slab(acc_x, flipped, pe.ext, 0, w1t, False)
    for k in (1, 2, 3):
        one(k).wait()
    total = s0[pl.ds(pos1 * QUART, QUART)].astype(F32)
    for k in range(3):
        total += r1[k].astype(F32)
    s1[...] = total.astype(BF)
    for k in (1, 2, 3):
        two(k).start()
    pe.arrive_rows(1)
    pe.arrive(1)

    @pl.loop(0, CELLS // BLK)
    def _(i):
        value = acc_x[rows_of(i)] + flipped(pe.ext, 2, i, w1t)
        dx_ref[rows_of(i)] = value[:, :C].astype(BF)
    for k in (1, 2, 3):
        two(k).wait()
    total = s1[pl.ds(pos2 * SIX, SIX)].astype(F32)
    for k in range(3):
        total += r2[k].astype(F32)
    r3[z] = total.astype(BF)
    for k in range(1, 8):
        three(k).start()
    for k in range(1, 8):
        three(k).wait_send()
        three_in(k).wait_recv()
    total = r3[0].astype(F32)
    for k in range(1, 8):
        total += r3[k].astype(F32)
    ff[core, pl.ds(pos1 * QUART + pos2 * SIX, SIX)] = total.astype(BF)
    for k in (1, 2, 3):
        four(k).start()
    for k in (1, 2, 3):
        four(k).wait_send()
        four_in(k).wait_recv()
    for k in (1, 2, 3):
        five(k).start()
    for k in (1, 2, 3):
        five(k).wait_send()
        five_in(k).wait_recv()
    back = remote(ff.at[core], ff.at[core], pair_sem2.at[0], pair_sem2.at[1], partner)
    back.start()
    xe.drain()
    ce.drain()
    pe.drain()
    back.wait_send()
    remote(ff.at[1 - core], ff.at[1 - core], pair_sem2.at[0], pair_sem2.at[1], partner).wait_recv()
    ff_ref[...] = ff[...]


def finish(scale, ff_ref, g1_ref, g2_ref):
    for which, out in ((0, g1_ref), (1, g2_ref)):
        @pl.loop(0, 9)
        def _(t):
            main = ff_ref[which, pl.ds(t * TAPU, 24)].astype(F32).reshape(C, 128) * scale
            tail = ff_ref[which, pl.ds(t * TAPU + 24, 12)].astype(F32).reshape(96, 128) * scale
            row = pl.multiple_of(t * C, C)
            out[pl.ds(row, C), 0:128] = main
            out[pl.ds(row, 96), 128:C] = tail[:, :64]
            out[pl.ds(row + 96, 96), 128:C] = tail[:, 64:]


def shards(n_lon, n_lat, inputs, cotangent, first_weight, second_weight):
    height, width, channels = inputs.shape
    scale = 1.0 / math.sqrt(height * n_lat * width * n_lon)
    vmem = pl.BlockSpec(memory_space=pltpu.VMEM)
    quarter, six = UNITS // 4, UNITS // 16
    dma = pltpu.SemaphoreType.DMA
    scratch = exchange_scratch() * 3 + [
        pltpu.VMEM((3, 3 * CP, CP), BF),
        pltpu.VMEM((3, CP, 3 * CP), BF),
        pltpu.VMEM((3, CP, 3 * CP), BF),
        pltpu.VMEM((CELLS, CP), F32),
        pltpu.VMEM((CELLS, CP), F32),
        pltpu.VMEM((CP, CELLS), BF),
        pltpu.VMEM((3, CP, EXT), BF),
        pltpu.VMEM((EXT + 2 * ROW, CP), BF),
        pltpu.VMEM((2, UNITS, 8, 128), BF),
        pltpu.VMEM((UNITS, 8, 128), BF),
        pltpu.VMEM((UNITS, 8, 128), BF),
        pltpu.VMEM((3, quarter, 8, 128), BF),
        pltpu.VMEM((quarter, 8, 128), BF),
        pltpu.VMEM((3, six, 8, 128), BF),
        pltpu.VMEM((8, six, 8, 128), BF),
        dma((2,)), dma((3,)), dma((3,)), dma((3,)), dma((3,)),
        dma((7,)), dma((7,)), dma((3,)), dma((3,)), dma((3,)), dma((3,)), dma((2,)),
        pltpu.VMEM((2, UNITS, 8, 128), BF),
    ]
    dx, ff = pl.pallas_call(
        functools.partial(kernel, n_lon, n_lat),
        out_shape=(jax.ShapeDtypeStruct((CELLS, C), BF),
                   jax.ShapeDtypeStruct((2, UNITS, 8, 128), BF)),
        in_specs=[vmem] * 4,
        out_specs=(vmem, vmem),
        scratch_shapes=scratch,
        compiler_params=pltpu.CompilerParams(collective_id=0, has_side_effects=True,
                                             vmem_limit_bytes=56 << 20),
        name="conv_grads",
    )(inputs.reshape(CELLS, C), cotangent.reshape(CELLS, C),
      first_weight.reshape(9, C, C), second_weight.reshape(9, C, C))
    g1, g2 = pl.pallas_call(
        functools.partial(finish, scale),
        out_shape=(jax.ShapeDtypeStruct((9 * C, C), F32),) * 2,
        in_specs=[vmem],
        out_specs=(vmem, vmem),
        name="unpack_grads",
    )(ff)
    return (dx.reshape(height, width, channels), g1.reshape(3, 3, C, C), g2.reshape(3, 3, C, C))


def solution(mesh):
    placed = (P("lat", "lon", None), P("lat", "lon", None), P(), P())
    return jax.shard_map(
        functools.partial(shards, mesh.shape["lon"], mesh.shape["lat"]),
        mesh=mesh,
        in_specs=placed,
        out_specs=(P("lat", "lon", None), P(), P()),
        check_vma=False,
    )
```

```python
import functools
import math

import jax
import jax.numpy as jnp
from jax import lax
from jax.experimental import pallas as pl
from jax.experimental.pallas import tpu as pltpu
from jax.sharding import PartitionSpec as P

MESH = pl.DeviceIdType.MESH
BF = jnp.bfloat16
F32 = jnp.float32
ROW = 32
CELLS = 1024
EXT = 1152
C = 192
CP = 256
BLK = 512
UNITS = 352
TAPU = 36


def pack_tail(tail):
    half = tail.shape[0] // 2
    return jnp.concatenate([tail[:half], tail[half:]], axis=1)


def unpack_tail(ref, slot, start, packed):
    n = packed.shape[0]
    zero = jnp.zeros((n, 64), packed.dtype)
    ref[slot, start:start + n, 128:256] = jnp.concatenate([packed[:, :64], zero], axis=1)
    ref[slot, start + n:start + 2 * n, 128:256] = jnp.concatenate([packed[:, 64:], zero], axis=1)


class Exchange:
    def __init__(self, bufs, source, dist, lon, lat, n_lon, n_lat):
        (self.tail, self.rows, self.tail_in, self.rows_in,
         self.send, self.recv, self.ext) = bufs
        self.source = source
        self.lat, self.n_lat = lat, n_lat
        self.lon, self.dist, self.n_lon = lon, dist, n_lon

    def target(self, k):
        if isinstance(k, int) and k == 2:
            return self.lon
        return lax.rem(self.lon + self.n_lon + self.dist * (1 - 2 * k), self.n_lon)

    def crosses(self, k):
        place = lax.rem(self.lon, 16)
        return place >= 16 - self.dist if k == 0 else place < self.dist

    def comes_across(self, k):
        return self.crosses(1 - k)

    def copy(self, src, dst, s, lon, lat):
        return pltpu.make_async_remote_copy(
            src_ref=src, dst_ref=dst, send_sem=self.send.at[s], recv_sem=self.recv.at[s],
            device_id={"lon": lon, "lat": lat}, device_id_type=MESH)

    def main_copy(self, k):
        return self.copy(self.source, self.ext.at[2 * k, pl.ds(ROW, CELLS), pl.ds(0, 128)],
                         k, self.target(k), self.lat)

    def tail_copy(self, k):
        return self.copy(self.tail, self.tail_in.at[k], 2 + k, self.target(k), self.lat)

    def row_copy(self, k, side):
        lat = jnp.minimum(self.lat + 1, self.n_lat - 1) if side == 0 else jnp.maximum(self.lat - 1, 0)
        return self.copy(self.rows.at[side], self.rows_in.at[2 * k + side],
                         4 + 2 * k + side, self.target(k), lat)

    def start_slabs(self, across):
        for k in (0, 1):
            @pl.when(self.crosses(k) == across)
            def _():
                self.tail_copy(k).start()
                self.main_copy(k).start()

    def fill_rows(self, last, first):
        for side, part in ((0, last), (1, first)):
            self.rows[side, 0:ROW] = part[:, :128]
            self.rows[side, ROW:] = pack_tail(part[:, 128:C])

    def start_rows(self):
        for k in range(3):
            @pl.when(self.lat < self.n_lat - 1)
            def _():
                self.row_copy(k, 0).start()

            @pl.when(self.lat > 0)
            def _():
                self.row_copy(k, 1).start()

    def arrive_rows(self, k):
        slot = 1 if isinstance(k, int) and k == 2 else 2 * k
        zero = jnp.zeros((ROW, CP), BF)
        for side, start, here in ((0, 0, self.lat > 0), (1, ROW + CELLS, self.lat < self.n_lat - 1)):
            @pl.when(here)
            def _():
                self.row_copy(k, side).wait_recv()
                packed = self.rows_in[2 * k + side]
                self.ext[slot, start:start + ROW, 0:128] = packed[:ROW]
                unpack_tail(self.ext, slot, start, packed[ROW:])

            @pl.when(jnp.logical_not(here))
            def _():
                self.ext[slot, start:start + ROW] = zero

    def arrive(self, k):
        self.tail_copy(k).wait_recv()
        unpack_tail(self.ext, 2 * k, ROW, self.tail_in[k])
        self.main_copy(k).wait_recv()

    def drain(self):
        for k in (0, 1):
            self.main_copy(k).wait_send()
            self.tail_copy(k).wait_send()
        for k in range(3):
            @pl.when(self.lat < self.n_lat - 1)
            def _():
                self.row_copy(k, 0).wait_send()

            @pl.when(self.lat > 0)
            def _():
                self.row_copy(k, 1).wait_send()


def exchange_scratch():
    return [
        pltpu.VMEM((CELLS // 2, 128), BF),
        pltpu.VMEM((2, ROW * 3 // 2, 128), BF),
        pltpu.VMEM((2, CELLS // 2, 128), BF),
        pltpu.VMEM((6, ROW * 3 // 2, 128), BF),
        pltpu.SemaphoreType.DMA((10,)),
        pltpu.SemaphoreType.DMA((10,)),
        pltpu.VMEM((3, EXT, CP), BF),
    ]


HALF, QUART, SIXTH = UNITS // 2, UNITS // 8, UNITS // 32


def remote(src, dst, ss, rs, dev):
    return pltpu.make_async_remote_copy(src_ref=src, dst_ref=dst, send_sem=ss, recv_sem=rs,
                                        device_id=dev, device_id_type=MESH)


class Chain:
    def __init__(self, w, part, ff, refs, core, pos1, pos2, z, partner, first, second, third):
        self.w, self.part, self.ff = w, part, ff
        (self.pair_in, self.s0, self.own0, self.r1, self.s1, self.own1, self.r2, self.r3,
         self.pair, self.sem1, self.sem2, self.sem3, self.sem4, self.sem5,
         self.sem6, self.spare) = refs
        self.core, self.pos1, self.pos2, self.z = core, pos1, pos2, z
        self.partner, self.first, self.second, self.third = partner, first, second, third

    def swap(self):
        return remote(self.part.at[self.w, pl.ds((1 - self.core) * HALF, HALF)], self.pair_in,
                      self.pair.at[0], self.pair.at[1], self.partner)

    def to_first(self, k):
        spot = self.s0.at[pl.ds(lax.rem(self.pos1 + k, 4) * QUART, QUART)]
        return remote(spot, self.r1.at[k - 1], self.sem1.at[0, k - 1], self.sem1.at[1, k - 1], self.first(k))

    def to_second(self, k):
        spot = self.s1.at[pl.ds(lax.rem(self.pos2 + k, 4) * SIXTH, SIXTH)]
        return remote(spot, self.r2.at[k - 1], self.sem2.at[0, k - 1], self.sem2.at[1, k - 1], self.second(k))

    def to_third(self, k, back=0):
        spot = self.r3.at[lax.rem(self.z + back, 8)]
        return remote(spot, spot, self.sem3.at[0, k - 1], self.sem3.at[1, k - 1], self.third(k))

    def place(self, p1, p2, size):
        return self.ff.at[self.w, pl.ds(self.core * HALF + p1 * QUART + p2 * SIXTH, size)]

    def piece(self, k, back=0):
        spot = self.place(self.pos1, lax.rem(self.pos2 + back, 4), SIXTH)
        return remote(spot, spot, self.sem4.at[0, k - 1], self.sem4.at[1, k - 1], self.second(k))

    def spread(self, k, j, back=0):
        spot = self.place(lax.rem(self.pos1 + back, 4), lax.rem(self.pos2 + 4 - j, 4), SIXTH)
        return remote(spot, spot, self.sem5.at[0, k - 1, j], self.sem5.at[1, k - 1, j], self.first(k))

    def back(self, k, theirs=False):
        core = 1 - self.core if theirs else self.core
        spot = self.ff.at[self.w, pl.ds(core * HALF + lax.rem(self.pos1 + 4 - k, 4) * QUART, QUART)]
        return remote(spot, spot, self.sem6.at[0, k], self.sem6.at[1, k], self.partner)

    def swap_start(self):
        self.swap().start()

    def swap_end(self):
        self.swap().wait()
        mine = self.part[self.w, pl.ds(self.core * HALF, HALF)].astype(F32) + self.pair_in[...].astype(F32)
        self.s0[...] = mine.astype(BF)
        for k in (1, 2, 3):
            self.to_first(k).start()

    def first_end(self):
        spot = pl.ds(self.pos1 * QUART, QUART)
        total = (self.part[self.w, pl.ds(self.core * HALF + self.pos1 * QUART, QUART)].astype(F32)
                 + self.pair_in[spot].astype(F32))
        for k in (1, 2, 3):
            self.to_first(k).wait()
            total += self.r1[k - 1].astype(F32)
        self.own1[...] = total
        self.s1[...] = total.astype(BF)
        for k in (1, 2, 3):
            self.to_second(k).start()

    def second_end(self):
        total = self.own1[pl.ds(self.pos2 * SIXTH, SIXTH)]
        for k in (1, 2, 3):
            self.to_second(k).wait()
            total += self.r2[k - 1].astype(F32)
        self.r3[self.z] = total.astype(BF)
        for k in range(1, 8):
            self.to_third(k).start()

    def third_end(self):
        for k in range(1, 8):
            self.to_third(k).wait_send()
            self.to_third(k, 8 - k).wait_recv()
        total = self.r3[0].astype(F32)
        for k in range(1, 8):
            total += self.r3[k].astype(F32)
        self.ff[self.w, pl.ds(self.core * HALF + self.pos1 * QUART + self.pos2 * SIXTH, SIXTH)] = total.astype(BF)
        for k in (1, 2, 3):
            self.piece(k).start()
        for k in (1, 2, 3):
            self.spread(k, 0).start()

    def gather_second(self):
        for j in (1, 2, 3):
            self.piece(j, 4 - j).wait_recv()
            for k in (1, 2, 3):
                self.spread(k, j).start()
        self.back(0).start()

    def gather_first(self):
        for k in (1, 2, 3):
            for j in range(4):
                self.spread(k, j, 4 - k).wait_recv()
            self.back(k).start()

    def back_end(self):
        for k in range(4):
            self.back(k, True).wait_recv()
        for k in range(4):
            self.back(k).wait_send()
        for k in (1, 2, 3):
            self.piece(k).wait_send()
            for j in range(4):
                self.spread(k, j).wait_send()


def kernel(n_lon, n_lat, x_ref, c_ref, w1_ref, w2_ref, dx_ref, ff_ref, *scratch):
    xb, cb, pb = scratch[0:7], scratch[7:14], scratch[14:21]
    (xv, cv, wv1, wv2, load_sem, w1n, w1t, w2t, acc_x, acc_c, hid_t, x_t, gz, part, dxv, out_sem,
     ff) = scratch[21:38]
    chains = (scratch[38:54], scratch[54:70])
    lon, lat = lax.axis_index("lon"), lax.axis_index("lat")
    core = lax.rem(lon, 2)
    z = lax.rem(lon // 2, 8)
    y = (lon // 16) * 2 + lax.rem(lat, 2)
    x = lat // 2

    def at(xx, yy, zz):
        return {"lon": (yy // 2) * 16 + zz * 2 + core, "lat": xx * 2 + lax.rem(yy, 2)}

    def first(k):
        return at(lax.rem(x + k * (1 - core), 4), lax.rem(y + k * core, 4), z)

    def second(k):
        return at(lax.rem(x + k * core, 4), lax.rem(y + k * (1 - core), 4), z)

    def third(k):
        return at(x, y, lax.rem(z + k, 8))

    partner = {"lon": lon + 1 - 2 * core, "lat": lat}
    pos1 = x * (1 - core) + y * core
    pos2 = y * (1 - core) + x * core

    barrier = pltpu.get_barrier_semaphore()

    def greet(dev):
        pl.semaphore_signal(barrier, inc=1, device_id=dev, device_id_type=MESH)

    for dl in (-2, -1, 1, 2):
        greet({"lon": lax.rem(lon + n_lon + dl, n_lon), "lat": lat})
    for da, here in ((-1, lat > 0), (1, lat < n_lat - 1)):
        @pl.when(here)
        def _():
            for dl in (-2, -1, 0, 1, 2):
                greet({"lon": lax.rem(lon + n_lon + dl, n_lon), "lat": lat + da})
    for k in (1, 2, 3):
        greet(first(k))
        greet(second(k))
    for k in range(1, 8):
        greet(third(k))

    xe = Exchange(xb, x_ref.at[:, pl.ds(0, 128)], 1, lon, lat, n_lon, n_lat)
    ce = Exchange(cb, c_ref.at[:, pl.ds(0, 128)], 2, lon, lat, n_lon, n_lat)
    pe = Exchange(pb, gz.at[pl.ds(2 * ROW, CELLS), pl.ds(0, 128)], 1, lon, lat, n_lon, n_lat)
    loads = [pltpu.make_async_copy(src, dst, load_sem.at[i]) for i, (src, dst) in enumerate(
        ((x_ref, xv), (c_ref, cv), (w1_ref, wv1), (w2_ref, wv2)))]
    for load in loads:
        load.start()
    for e, v, load in ((xe, xv, loads[0]), (ce, cv, loads[1])):
        load.wait()
        e.fill_rows(v[CELLS - ROW:], v[:ROW])
    xe.tail[...] = pack_tail(xv[:, 128:C])
    beside = jnp.where(lat > 0, 5, 0) + jnp.where(lat < n_lat - 1, 5, 0)
    pl.semaphore_wait(barrier, 4 + 6 + 7 + beside)
    xe.start_rows()
    ce.start_rows()
    xe.start_slabs(False)
    ce.tail[...] = pack_tail(cv[:, 128:C])

    w1n[...] = jnp.zeros_like(w1n)
    w1t[...] = jnp.zeros_like(w1t)
    w2t[...] = jnp.zeros_like(w2t)
    gz[0:2 * ROW] = jnp.zeros((2 * ROW, CP), BF)
    gz[2 * ROW + CELLS:] = jnp.zeros((gz.shape[0] - 2 * ROW - CELLS, CP), BF)
    for e, v in ((xe, xv), (ce, cv)):
        e.ext[1, ROW:ROW + CELLS, 0:128] = v[:, :128]
        e.ext[1, ROW:ROW + CELLS, 128:256] = jnp.concatenate(
            [v[:, 128:C], jnp.zeros((CELLS, 64), BF)], axis=1)
    for w in (0, 1):
        part[w, 324:] = jnp.zeros((UNITS - 324, 8, 128), BF)
    for slot in range(3):
        xe.ext[slot, 2 * ROW + CELLS:] = jnp.zeros((EXT - 2 * ROW - CELLS, CP), BF)
    loads[2].wait()
    loads[3].wait()
    for b in range(3):
        for a in range(3):
            w1n[b, a * CP:a * CP + C, 0:C] = wv1[a * 3 + b]
            w1t[b, 0:C, a * CP:a * CP + C] = wv1[(2 - a) * 3 + 2 - b]
            w2t[b, 0:C, a * CP:a * CP + C] = wv2[(2 - a) * 3 + 2 - b]

    def taps(ext, slot, i):
        start = pl.multiple_of(i * BLK, BLK)
        return jnp.concatenate([ext[slot, pl.ds(start + a * ROW, BLK), :] for a in range(3)], axis=1)

    def straight(ext, slot, i, w):
        return jnp.dot(taps(ext, slot, i), w[slot], preferred_element_type=F32)

    def flipped(ext, slot, i, w):
        return lax.dot_general(taps(ext, slot, i), w[slot], (((1,), (1,)), ((), ())),
                               preferred_element_type=F32)

    def rows_of(i):
        return pl.ds(pl.multiple_of(i * BLK, BLK), BLK)

    def add_slab(acc, conv, ext, slot, w, new):
        @pl.loop(0, CELLS // BLK)
        def _(i):
            value = conv(ext, slot, i, w)
            acc[rows_of(i)] = value if new else acc[rows_of(i)] + value

    def put_tap(which, tap, grad):
        main = grad[:, :128].reshape(24, 8, 128)
        tail = jnp.concatenate([grad[:96, 128:C], grad[96:, 128:C]], axis=1).reshape(12, 8, 128)
        part[which, pl.ds(tap * TAPU, 24)] = main.astype(BF)
        part[which, pl.ds(tap * TAPU + 24, 12)] = tail.astype(BF)

    ce.start_slabs(False)
    xe.arrive_rows(2)
    ce.arrive_rows(2)
    xe.start_slabs(True)
    ce.start_slabs(True)
    add_slab(acc_x, straight, xe.ext, 1, w1n, True)
    x_t[1] = xe.ext[1].T

    def take_x(k):
        xe.arrive_rows(k)
        xe.arrive(k)
        add_slab(acc_x, straight, xe.ext, 2 * k, w1n, False)
        x_t[2 * k] = xe.ext[2 * k].T

    take_x(1 - core)
    add_slab(acc_c, flipped, ce.ext, 1, w2t, True)
    take_x(core)

    @pl.loop(0, CELLS // BLK)
    def _(i):
        pre = acc_x[rows_of(i)]
        sig = 1.0 / (1.0 + jnp.exp(-pre))
        hid_t[:, rows_of(i)] = (pre * sig).astype(BF).T
        acc_x[rows_of(i)] = sig * (1.0 + pre * (1.0 - sig))

    def second_grad(slot):
        @pl.loop(0, 3)
        def _(a):
            rhs = ce.ext[slot, pl.ds(pl.multiple_of((2 - a) * ROW, ROW), CELLS), :]
            put_tap(1, a * 3 + 2 - slot, jnp.dot(hid_t[0:C], rhs, preferred_element_type=F32))

    second_grad(1)
    for k in (0, 1):
        ce.arrive_rows(k)
        ce.arrive(k)
        add_slab(acc_c, flipped, ce.ext, 2 * k, w2t, False)

    @pl.loop(0, CELLS // BLK)
    def _(i):
        value = (acc_c[rows_of(i)] * acc_x[rows_of(i)]).astype(BF)
        gz[pl.ds(pl.multiple_of(i * BLK + 2 * ROW, 2 * ROW), BLK)] = value
        pe.ext[1, pl.ds(pl.multiple_of(i * BLK + ROW, ROW), BLK)] = value
    pe.fill_rows(gz[CELLS + ROW:CELLS + 2 * ROW], gz[2 * ROW:3 * ROW])
    pe.start_rows()
    pe.tail[...] = pack_tail(gz[2 * ROW:2 * ROW + CELLS, 128:C])
    pe.start_slabs(False)

    @pl.loop(0, 3)
    def _(a):
        rhs = gz[pl.ds(pl.multiple_of((2 - a) * ROW, ROW), EXT), :]
        for b in range(3):
            put_tap(0, a * 3 + b, jnp.dot(x_t[b, 0:C], rhs, preferred_element_type=F32))

    one, two = (Chain(w, part, ff, refs, core, pos1, pos2, z, partner, first, second, third)
                for w, refs in enumerate(chains))
    one.swap_start()
    second_grad(0)
    second_grad(2)
    two.swap_start()
    one.swap_end()
    pe.arrive_rows(2)
    add_slab(acc_x, flipped, pe.ext, 1, w1t, True)
    two.swap_end()

    def take_p(k, across):
        @pl.when(pe.comes_across(k) == across)
        def _():
            pe.arrive_rows(k)
            pe.arrive(k)
            add_slab(acc_x, flipped, pe.ext, 2 * k, w1t, False)

    take_p(0, False)
    one.first_end()
    take_p(1, False)
    two.first_end()
    one.second_end()
    two.second_end()
    pe.start_slabs(True)
    xe.drain()
    ce.drain()
    one.third_end()
    two.third_end()
    take_p(0, True)
    take_p(1, True)
    one.gather_second()
    two.gather_second()
    one.gather_first()
    two.gather_first()

    @pl.loop(0, CELLS // BLK)
    def _(i):
        dxv[rows_of(i)] = acc_x[rows_of(i), 0:C].astype(BF)
    dx_out = pltpu.make_async_copy(dxv, dx_ref, out_sem.at[0])
    dx_out.start()
    pe.drain()
    outs = []
    for chain in (one, two):
        chain.back_end()
        out = pltpu.make_async_copy(ff.at[chain.w], ff_ref.at[chain.w], out_sem.at[1 + chain.w])
        out.start()
        outs.append(out)
    for out in outs:
        out.wait()
    dx_out.wait()


def finish(scale, ff_ref, dx_ref, g1_ref, g2_ref, out_ref, ffv, gv, dxv, sem_in, sem_out):
    parts = [(j, which) for j in range(3) for which in (0, 1)]

    def take(j, which):
        units = pl.ds(j * 3 * TAPU, 3 * TAPU)
        return pltpu.make_async_copy(ff_ref.at[which, units], ffv.at[which, units], sem_in.at[which, j])

    def give(j, which):
        rows = pl.ds(j * 3 * C, 3 * C)
        return pltpu.make_async_copy(gv.at[which, rows], (g1_ref, g2_ref)[which].at[rows], sem_out.at[which, j])

    dx_in = pltpu.make_async_copy(dx_ref, dxv, sem_in.at[0, 3])
    dx_out = pltpu.make_async_copy(dxv, out_ref, sem_out.at[0, 3])
    for part in parts:
        take(*part).start()
    dx_in.start()
    for j, which in parts:
        take(j, which).wait()
        for t in range(3 * j, 3 * j + 3):
            main = ffv[which, t * TAPU:t * TAPU + 24].astype(F32).reshape(C, 128) * scale
            tail = ffv[which, t * TAPU + 24:(t + 1) * TAPU].astype(F32).reshape(96, 128) * scale
            row = t * C
            gv[which, row:row + C, 0:128] = main
            gv[which, row:row + 96, 128:C] = tail[:, :64]
            gv[which, row + 96:row + C, 128:C] = tail[:, 64:]
        give(j, which).start()
        if (j, which) == (0, 1):
            dx_in.wait()
            dx_out.start()
    for part in parts:
        give(*part).wait()
    dx_out.wait()


def shards(n_lon, n_lat, inputs, cotangent, first_weight, second_weight):
    height, width, channels = inputs.shape
    scale = 1.0 / math.sqrt(height * n_lat * width * n_lon)
    dma = pltpu.SemaphoreType.DMA
    scratch = exchange_scratch() * 3 + [
        pltpu.VMEM((CELLS, C), BF),
        pltpu.VMEM((CELLS, C), BF),
        pltpu.VMEM((9, C, C), BF),
        pltpu.VMEM((9, C, C), BF),
        dma((4,)),
        pltpu.VMEM((3, 3 * CP, CP), BF),
        pltpu.VMEM((3, CP, 3 * CP), BF),
        pltpu.VMEM((3, CP, 3 * CP), BF),
        pltpu.VMEM((CELLS, CP), F32),
        pltpu.VMEM((CELLS, CP), F32),
        pltpu.VMEM((CP, CELLS), BF),
        pltpu.VMEM((3, CP, EXT), BF),
        pltpu.VMEM((EXT + 2 * ROW, CP), BF),
        pltpu.VMEM((2, UNITS, 8, 128), BF),
        pltpu.VMEM((CELLS, C), BF),
        dma((3,)),
        pltpu.VMEM((2, UNITS, 8, 128), BF),
    ] + [
        pltpu.VMEM((HALF, 8, 128), BF),
        pltpu.VMEM((HALF, 8, 128), BF),
        pltpu.VMEM((8, 128), F32),
        pltpu.VMEM((3, QUART, 8, 128), BF),
        pltpu.VMEM((QUART, 8, 128), BF),
        pltpu.VMEM((QUART, 8, 128), F32),
        pltpu.VMEM((3, SIXTH, 8, 128), BF),
        pltpu.VMEM((8, SIXTH, 8, 128), BF),
        dma((2,)), dma((2, 3)), dma((2, 3)), dma((2, 7)), dma((2, 3)), dma((2, 3, 4)),
        dma((2, 4)), dma((1,)),
    ] * 2
    dx, ff = pl.pallas_call(
        functools.partial(kernel, n_lon, n_lat),
        out_shape=(jax.ShapeDtypeStruct((CELLS, C), BF),
                   jax.ShapeDtypeStruct((2, UNITS, 8, 128), BF)),
        in_specs=[pl.BlockSpec(memory_space=pl.ANY)] * 4,
        out_specs=(pl.BlockSpec(memory_space=pl.ANY),) * 2,
        scratch_shapes=scratch,
        compiler_params=pltpu.CompilerParams(collective_id=0, has_side_effects=True,
                                             vmem_limit_bytes=60 << 20),
        name="conv_grads",
    )(inputs.reshape(CELLS, C), cotangent.reshape(CELLS, C),
      first_weight.reshape(9, C, C), second_weight.reshape(9, C, C))
    anywhere = pl.BlockSpec(memory_space=pl.ANY)
    g1, g2, dx = pl.pallas_call(
        functools.partial(finish, scale),
        out_shape=(jax.ShapeDtypeStruct((9 * C, C), F32),) * 2 + (jax.ShapeDtypeStruct((CELLS, C), BF),),
        in_specs=[anywhere] * 2,
        out_specs=(anywhere,) * 3,
        scratch_shapes=[
            pltpu.VMEM((2, UNITS, 8, 128), BF),
            pltpu.VMEM((2, 9 * C, C), F32),
            pltpu.VMEM((CELLS, C), BF),
            dma((2, 4)),
            dma((2, 4)),
        ],
        compiler_params=pltpu.CompilerParams(vmem_limit_bytes=60 << 20),
        name="unpack_grads",
    )(ff, dx)
    return (dx.reshape(height, width, channels), g1.reshape(3, 3, C, C), g2.reshape(3, 3, C, C))


def solution(mesh):
    placed = (P("lat", "lon", None), P("lat", "lon", None), P(), P())
    return jax.shard_map(
        functools.partial(shards, mesh.shape["lon"], mesh.shape["lat"]),
        mesh=mesh,
        in_specs=placed,
        out_specs=(P("lat", "lon", None), P(), P()),
        check_vma=False,
    )
```

```python
import functools
import math

import jax
import jax.numpy as jnp
from jax import lax
from jax.experimental import pallas as pl
from jax.experimental.pallas import tpu as pltpu
from jax.sharding import PartitionSpec as P

MESH = pl.DeviceIdType.MESH
BF = jnp.bfloat16
F32 = jnp.float32
ROW = 32
CELLS = 1024
EXT = 1152
C = 192
CP = 256
BLK = 512
UNITS = 352
TAPU = 36


def pack_tail(tail):
    half = tail.shape[0] // 2
    return jnp.concatenate([tail[:half], tail[half:]], axis=1)


def unpack_tail(ref, slot, start, packed):
    n = packed.shape[0]
    zero = jnp.zeros((n, 64), packed.dtype)
    ref[slot, start:start + n, 128:256] = jnp.concatenate([packed[:, :64], zero], axis=1)
    ref[slot, start + n:start + 2 * n, 128:256] = jnp.concatenate([packed[:, 64:], zero], axis=1)


class Exchange:
    def __init__(self, bufs, source, dist, lon, lat, n_lon, n_lat):
        (self.tail, self.rows, self.tail_in, self.rows_in,
         self.send, self.recv, self.ext) = bufs
        self.source = source
        self.lat, self.n_lat = lat, n_lat
        self.lon, self.dist, self.n_lon = lon, dist, n_lon

    def target(self, k):
        if isinstance(k, int) and k == 2:
            return self.lon
        return lax.rem(self.lon + self.n_lon + self.dist * (1 - 2 * k), self.n_lon)

    def crosses(self, k):
        place = lax.rem(self.lon, 16)
        return place >= 16 - self.dist if k == 0 else place < self.dist

    def comes_across(self, k):
        return self.crosses(1 - k)

    def copy(self, src, dst, s, lon, lat):
        return pltpu.make_async_remote_copy(
            src_ref=src, dst_ref=dst, send_sem=self.send.at[s], recv_sem=self.recv.at[s],
            device_id={"lon": lon, "lat": lat}, device_id_type=MESH)

    def main_copy(self, k):
        return self.copy(self.source, self.ext.at[2 * k, pl.ds(ROW, CELLS), pl.ds(0, 128)],
                         k, self.target(k), self.lat)

    def tail_copy(self, k):
        return self.copy(self.tail, self.tail_in.at[k], 2 + k, self.target(k), self.lat)

    def row_copy(self, side):
        lat = jnp.minimum(self.lat + 1, self.n_lat - 1) if side == 0 else jnp.maximum(self.lat - 1, 0)
        return self.copy(self.rows.at[side], self.rows_in.at[4 + side], 4 + side, self.lon, lat)

    def pass_copy(self, k, side):
        return self.copy(self.rows_in.at[4 + side], self.rows_in.at[2 * k + side],
                         6 + 2 * k + side, self.target(k), self.lat)

    def has_row(self, side):
        return self.lat > 0 if side == 0 else self.lat < self.n_lat - 1

    def sends_row(self, side):
        return self.has_row(1 - side)

    def start_slabs(self, across):
        for k in (0, 1):
            @pl.when(self.crosses(k) == across)
            def _():
                self.tail_copy(k).start()
                self.main_copy(k).start()

    def fill_rows(self, last, first):
        for side, part in ((0, last), (1, first)):
            self.rows[side, 0:ROW] = part[:, :128]
            self.rows[side, ROW:] = pack_tail(part[:, 128:C])

    def start_rows(self):
        for side in (0, 1):
            @pl.when(self.sends_row(side))
            def _():
                self.row_copy(side).start()

    def own_rows(self):
        for side in (0, 1):
            @pl.when(self.has_row(side))
            def _():
                self.row_copy(side).wait_recv()
                for k in (0, 1):
                    self.pass_copy(k, side).start()
        self.place_rows(2, 1)

    def place_rows(self, k, slot):
        zero = jnp.zeros((ROW, CP), BF)
        for side, start in ((0, 0), (1, ROW + CELLS)):
            @pl.when(self.has_row(side))
            def _():
                packed = self.rows_in[2 * k + side]
                self.ext[slot, start:start + ROW, 0:128] = packed[:ROW]
                unpack_tail(self.ext, slot, start, packed[ROW:])

            @pl.when(jnp.logical_not(self.has_row(side)))
            def _():
                self.ext[slot, start:start + ROW] = zero

    def arrive_rows(self, k):
        for side in (0, 1):
            @pl.when(self.has_row(side))
            def _():
                self.pass_copy(k, side).wait_recv()
        self.place_rows(k, 2 * k)

    def arrive(self, k):
        self.tail_copy(k).wait_recv()
        unpack_tail(self.ext, 2 * k, ROW, self.tail_in[k])
        self.main_copy(k).wait_recv()

    def drain(self):
        for k in (0, 1):
            self.main_copy(k).wait_send()
            self.tail_copy(k).wait_send()
        for side in (0, 1):
            @pl.when(self.sends_row(side))
            def _():
                self.row_copy(side).wait_send()

            @pl.when(self.has_row(side))
            def _():
                for k in (0, 1):
                    self.pass_copy(k, side).wait_send()


def exchange_scratch():
    return [
        pltpu.VMEM((CELLS // 2, 128), BF),
        pltpu.VMEM((2, ROW * 3 // 2, 128), BF),
        pltpu.VMEM((2, CELLS // 2, 128), BF),
        pltpu.VMEM((6, ROW * 3 // 2, 128), BF),
        pltpu.SemaphoreType.DMA((10,)),
        pltpu.SemaphoreType.DMA((10,)),
        pltpu.VMEM((3, EXT, CP), BF),
    ]


HALF, QUART, SIXTH = UNITS // 2, UNITS // 8, UNITS // 32


def remote(src, dst, ss, rs, dev):
    return pltpu.make_async_remote_copy(src_ref=src, dst_ref=dst, send_sem=ss, recv_sem=rs,
                                        device_id=dev, device_id_type=MESH)


class Chain:
    def __init__(self, w, part, ff, out, refs, core, pos1, pos2, z, partner, first, second, third):
        self.w, self.part, self.ff, self.out = w, part, ff, out
        (self.pair_in, self.s0, self.own0, self.r1, self.s1, self.own1, self.r2, self.r3,
         self.pair, self.sem1, self.sem2, self.sem3, self.sem4, self.sem5,
         self.sem6, self.sem7) = refs
        self.core, self.pos1, self.pos2, self.z = core, pos1, pos2, z
        self.partner, self.first, self.second, self.third = partner, first, second, third

    def swap(self):
        return remote(self.part.at[self.w, pl.ds((1 - self.core) * HALF, HALF)], self.pair_in,
                      self.pair.at[0], self.pair.at[1], self.partner)

    def to_first(self, k):
        spot = self.s0.at[pl.ds(lax.rem(self.pos1 + k, 4) * QUART, QUART)]
        return remote(spot, self.r1.at[k - 1], self.sem1.at[0, k - 1], self.sem1.at[1, k - 1], self.first(k))

    def to_second(self, k):
        spot = self.s1.at[pl.ds(lax.rem(self.pos2 + k, 4) * SIXTH, SIXTH)]
        return remote(spot, self.r2.at[k - 1], self.sem2.at[0, k - 1], self.sem2.at[1, k - 1], self.second(k))

    def to_third(self, k, back=0):
        spot = self.r3.at[lax.rem(self.z + back, 8)]
        return remote(spot, spot, self.sem3.at[0, k - 1], self.sem3.at[1, k - 1], self.third(k))

    def place(self, p1, p2, size):
        return self.ff.at[self.w, pl.ds(self.core * HALF + p1 * QUART + p2 * SIXTH, size)]

    def piece(self, k, back=0):
        spot = self.place(self.pos1, lax.rem(self.pos2 + back, 4), SIXTH)
        return remote(spot, spot, self.sem4.at[0, k - 1], self.sem4.at[1, k - 1], self.second(k))

    def spread(self, k, j, back=0):
        spot = self.place(lax.rem(self.pos1 + back, 4), lax.rem(self.pos2 + 4 - j, 4), SIXTH)
        return remote(spot, spot, self.sem5.at[0, k - 1, j], self.sem5.at[1, k - 1, j], self.first(k))

    def back(self, k, theirs=False):
        core = 1 - self.core if theirs else self.core
        spot = pl.ds(core * HALF + lax.rem(self.pos1 + 4 - k, 4) * QUART, QUART)
        return remote(self.ff.at[self.w, spot], self.out.at[self.w, spot],
                      self.sem6.at[0, k], self.sem6.at[1, k], self.partner)

    def keep(self, k):
        spot = pl.ds(self.core * HALF + lax.rem(self.pos1 + 4 - k, 4) * QUART, QUART)
        return pltpu.make_async_copy(self.ff.at[self.w, spot], self.out.at[self.w, spot], self.sem7.at[k])

    def swap_start(self):
        self.swap().start()

    def swap_end(self):
        self.swap().wait()
        mine = self.part[self.w, pl.ds(self.core * HALF, HALF)].astype(F32) + self.pair_in[...].astype(F32)
        self.s0[...] = mine.astype(BF)
        for k in (1, 2, 3):
            self.to_first(k).start()

    def first_end(self):
        spot = pl.ds(self.pos1 * QUART, QUART)
        total = (self.part[self.w, pl.ds(self.core * HALF + self.pos1 * QUART, QUART)].astype(F32)
                 + self.pair_in[spot].astype(F32))
        for k in (1, 2, 3):
            self.to_first(k).wait()
            total += self.r1[k - 1].astype(F32)
        self.own1[...] = total
        self.s1[...] = total.astype(BF)
        for k in (1, 2, 3):
            self.to_second(k).start()

    def second_end(self):
        total = self.own1[pl.ds(self.pos2 * SIXTH, SIXTH)]
        for k in (1, 2, 3):
            self.to_second(k).wait()
            total += self.r2[k - 1].astype(F32)
        self.r3[self.z] = total.astype(BF)
        for k in range(1, 8):
            self.to_third(k).start()

    def third_end(self):
        for k in range(1, 8):
            self.to_third(k).wait_send()
            self.to_third(k, 8 - k).wait_recv()
        total = self.r3[0].astype(F32)
        for k in range(1, 8):
            total += self.r3[k].astype(F32)
        self.ff[self.w, pl.ds(self.core * HALF + self.pos1 * QUART + self.pos2 * SIXTH, SIXTH)] = total.astype(BF)
        for k in (1, 2, 3):
            self.piece(k).start()
        for k in (1, 2, 3):
            self.spread(k, 0).start()

    def gather_second(self):
        for j in (1, 2, 3):
            self.piece(j, 4 - j).wait_recv()
            for k in (1, 2, 3):
                self.spread(k, j).start()
        self.back(0).start()
        self.keep(0).start()

    def gather_first(self):
        for k in (1, 2, 3):
            for j in range(4):
                self.spread(k, j, 4 - k).wait_recv()
            self.back(k).start()
            self.keep(k).start()

    def back_end(self):
        for k in range(4):
            self.back(k, True).wait_recv()
            self.keep(k).wait()
        for k in range(4):
            self.back(k).wait_send()
        for k in (1, 2, 3):
            self.piece(k).wait_send()
            for j in range(4):
                self.spread(k, j).wait_send()


def kernel(n_lon, n_lat, x_ref, c_ref, w1_ref, w2_ref, dx_ref, ff_ref, *scratch):
    xb, cb, pb = scratch[0:7], scratch[7:14], scratch[14:21]
    (xv, cv, wv1, wv2, load_sem, w1n, w1t, w2t, acc_x, acc_c, hid_t, x_t, gz, part, dxv, out_sem,
     ff) = scratch[21:38]
    chains = (scratch[38:54], scratch[54:70])
    lon, lat = lax.axis_index("lon"), lax.axis_index("lat")
    core = lax.rem(lon, 2)
    z = lax.rem(lon // 2, 8)
    y = (lon // 16) * 2 + lax.rem(lat, 2)
    x = lat // 2

    def at(xx, yy, zz):
        return {"lon": (yy // 2) * 16 + zz * 2 + core, "lat": xx * 2 + lax.rem(yy, 2)}

    def first(k):
        return at(lax.rem(x + k * (1 - core), 4), lax.rem(y + k * core, 4), z)

    def second(k):
        return at(lax.rem(x + k * core, 4), lax.rem(y + k * (1 - core), 4), z)

    def third(k):
        return at(x, y, lax.rem(z + k, 8))

    partner = {"lon": lon + 1 - 2 * core, "lat": lat}
    pos1 = x * (1 - core) + y * core
    pos2 = y * (1 - core) + x * core

    barrier = pltpu.get_barrier_semaphore()

    def greet(dev):
        pl.semaphore_signal(barrier, inc=1, device_id=dev, device_id_type=MESH)

    for dl in (-2, -1, 1, 2):
        greet({"lon": lax.rem(lon + n_lon + dl, n_lon), "lat": lat})
    for da, here in ((-1, lat > 0), (1, lat < n_lat - 1)):
        @pl.when(here)
        def _():
            greet({"lon": lon, "lat": lat + da})
    for k in (1, 2, 3):
        greet(first(k))
        greet(second(k))
    for k in range(1, 8):
        greet(third(k))

    xe = Exchange(xb, x_ref.at[:, pl.ds(0, 128)], 1, lon, lat, n_lon, n_lat)
    ce = Exchange(cb, c_ref.at[:, pl.ds(0, 128)], 2, lon, lat, n_lon, n_lat)
    pe = Exchange(pb, gz.at[pl.ds(2 * ROW, CELLS), pl.ds(0, 128)], 1, lon, lat, n_lon, n_lat)
    loads = [pltpu.make_async_copy(src, dst, load_sem.at[i]) for i, (src, dst) in enumerate(
        ((x_ref, xv), (c_ref, cv), (w1_ref, wv1), (w2_ref, wv2)))]
    for load in loads:
        load.start()
    for e, v, load in ((xe, xv, loads[0]), (ce, cv, loads[1])):
        load.wait()
        e.fill_rows(v[CELLS - ROW:], v[:ROW])
    xe.tail[...] = pack_tail(xv[:, 128:C])
    beside = jnp.where(lat > 0, 1, 0) + jnp.where(lat < n_lat - 1, 1, 0)
    pl.semaphore_wait(barrier, 4 + 6 + 7 + beside)
    xe.start_rows()
    ce.start_rows()
    xe.start_slabs(False)
    ce.tail[...] = pack_tail(cv[:, 128:C])

    w1n[...] = jnp.zeros_like(w1n)
    w1t[...] = jnp.zeros_like(w1t)
    w2t[...] = jnp.zeros_like(w2t)
    gz[0:2 * ROW] = jnp.zeros((2 * ROW, CP), BF)
    gz[2 * ROW + CELLS:] = jnp.zeros((gz.shape[0] - 2 * ROW - CELLS, CP), BF)
    for e, v in ((xe, xv), (ce, cv)):
        e.ext[1, ROW:ROW + CELLS, 0:128] = v[:, :128]
        e.ext[1, ROW:ROW + CELLS, 128:256] = jnp.concatenate(
            [v[:, 128:C], jnp.zeros((CELLS, 64), BF)], axis=1)
    for w in (0, 1):
        part[w, 324:] = jnp.zeros((UNITS - 324, 8, 128), BF)
    for slot in range(3):
        xe.ext[slot, 2 * ROW + CELLS:] = jnp.zeros((EXT - 2 * ROW - CELLS, CP), BF)
    loads[2].wait()
    loads[3].wait()
    for b in range(3):
        for a in range(3):
            w1n[b, a * CP:a * CP + C, 0:C] = wv1[a * 3 + b]
            w1t[b, 0:C, a * CP:a * CP + C] = wv1[(2 - a) * 3 + 2 - b]
            w2t[b, 0:C, a * CP:a * CP + C] = wv2[(2 - a) * 3 + 2 - b]

    def taps(ext, slot, i):
        start = pl.multiple_of(i * BLK, BLK)
        return jnp.concatenate([ext[slot, pl.ds(start + a * ROW, BLK), :] for a in range(3)], axis=1)

    def straight(ext, slot, i, w):
        return jnp.dot(taps(ext, slot, i), w[slot], preferred_element_type=F32)

    def flipped(ext, slot, i, w):
        return lax.dot_general(taps(ext, slot, i), w[slot], (((1,), (1,)), ((), ())),
                               preferred_element_type=F32)

    def rows_of(i):
        return pl.ds(pl.multiple_of(i * BLK, BLK), BLK)

    def add_slab(acc, conv, ext, slot, w, new):
        @pl.loop(0, CELLS // BLK)
        def _(i):
            value = conv(ext, slot, i, w)
            acc[rows_of(i)] = value if new else acc[rows_of(i)] + value

    def put_tap(which, tap, grad):
        main = grad[:, :128].reshape(24, 8, 128)
        tail = jnp.concatenate([grad[:96, 128:C], grad[96:, 128:C]], axis=1).reshape(12, 8, 128)
        part[which, pl.ds(tap * TAPU, 24)] = main.astype(BF)
        part[which, pl.ds(tap * TAPU + 24, 12)] = tail.astype(BF)

    xe.own_rows()
    ce.own_rows()
    xe.start_slabs(True)
    ce.start_slabs(False)
    ce.start_slabs(True)
    add_slab(acc_x, straight, xe.ext, 1, w1n, True)
    x_t[1] = xe.ext[1].T

    def take_x(k):
        xe.arrive_rows(k)
        xe.arrive(k)
        add_slab(acc_x, straight, xe.ext, 2 * k, w1n, False)
        x_t[2 * k] = xe.ext[2 * k].T

    take_x(1 - core)
    add_slab(acc_c, flipped, ce.ext, 1, w2t, True)
    take_x(core)

    @pl.loop(0, CELLS // BLK)
    def _(i):
        pre = acc_x[rows_of(i)]
        sig = 1.0 / (1.0 + jnp.exp(-pre))
        hid_t[:, rows_of(i)] = (pre * sig).astype(BF).T
        acc_x[rows_of(i)] = sig * (1.0 + pre * (1.0 - sig))

    def second_grad(slot):
        @pl.loop(0, 3)
        def _(a):
            rhs = ce.ext[slot, pl.ds(pl.multiple_of((2 - a) * ROW, ROW), CELLS), :]
            put_tap(1, a * 3 + 2 - slot, jnp.dot(hid_t[0:C], rhs, preferred_element_type=F32))

    second_grad(1)
    late = jnp.where(ce.comes_across(0), 0, 1)
    for k in (1 - late, late):
        ce.arrive_rows(k)
        ce.arrive(k)
        add_slab(acc_c, flipped, ce.ext, 2 * k, w2t, False)

    @pl.loop(0, CELLS // BLK)
    def _(i):
        value = (acc_c[rows_of(i)] * acc_x[rows_of(i)]).astype(BF)
        gz[pl.ds(pl.multiple_of(i * BLK + 2 * ROW, 2 * ROW), BLK)] = value
        pe.ext[1, pl.ds(pl.multiple_of(i * BLK + ROW, ROW), BLK)] = value
    pe.fill_rows(gz[CELLS + ROW:CELLS + 2 * ROW], gz[2 * ROW:3 * ROW])
    pe.start_rows()
    pe.tail[...] = pack_tail(gz[2 * ROW:2 * ROW + CELLS, 128:C])
    pe.start_slabs(False)

    @pl.loop(0, 3)
    def _(a):
        rhs = gz[pl.ds(pl.multiple_of((2 - a) * ROW, ROW), EXT), :]
        for b in range(3):
            put_tap(0, a * 3 + b, jnp.dot(x_t[b, 0:C], rhs, preferred_element_type=F32))

    one, two = (Chain(w, part, ff, ff_ref, refs, core, pos1, pos2, z, partner, first, second, third)
                for w, refs in enumerate(chains))
    one.swap_start()
    second_grad(0)
    second_grad(2)
    two.swap_start()
    one.swap_end()
    pe.own_rows()
    add_slab(acc_x, flipped, pe.ext, 1, w1t, True)
    two.swap_end()

    def take_p(k, across):
        @pl.when(pe.comes_across(k) == across)
        def _():
            pe.arrive_rows(k)
            pe.arrive(k)
            add_slab(acc_x, flipped, pe.ext, 2 * k, w1t, False)

    take_p(0, False)
    one.first_end()
    take_p(1, False)
    two.first_end()
    one.second_end()
    two.second_end()
    pe.start_slabs(True)
    xe.drain()
    ce.drain()
    one.third_end()
    two.third_end()
    one.gather_second()
    two.gather_second()
    take_p(0, True)
    take_p(1, True)
    one.gather_first()
    two.gather_first()

    @pl.loop(0, CELLS // BLK)
    def _(i):
        dxv[rows_of(i)] = acc_x[rows_of(i), 0:C].astype(BF)
    dx_out = pltpu.make_async_copy(dxv, dx_ref, out_sem.at[0])
    dx_out.start()
    pe.drain()
    for chain in (one, two):
        chain.back_end()
    dx_out.wait()


def finish(scale, ffv, dxv, g1_ref, g2_ref, out_ref, gv, sem_out):
    taps = [(t, which) for t in (0, 3, 6) for which in (0, 1)]

    def give(t, which):
        rows = pl.ds(t * C, 3 * C)
        return pltpu.make_async_copy(gv.at[which, rows], (g1_ref, g2_ref)[which].at[rows], sem_out.at[which, t])

    dx_out = pltpu.make_async_copy(dxv, out_ref, sem_out.at[0, 9])
    dx_out.start()
    for t, which in taps:
        for u in range(t, t + 3):
            main = ffv[which, u * TAPU:u * TAPU + 24].astype(F32).reshape(C, 128) * scale
            tail = ffv[which, u * TAPU + 24:(u + 1) * TAPU].astype(F32).reshape(96, 128) * scale
            row = u * C
            gv[which, row:row + C, 0:128] = main
            gv[which, row:row + 96, 128:C] = tail[:, :64]
            gv[which, row + 96:row + C, 128:C] = tail[:, 64:]
        give(t, which).start()
    for tap in taps:
        give(*tap).wait()
    dx_out.wait()


def shards(n_lon, n_lat, inputs, cotangent, first_weight, second_weight):
    height, width, channels = inputs.shape
    scale = 1.0 / math.sqrt(height * n_lat * width * n_lon)
    dma = pltpu.SemaphoreType.DMA
    scratch = exchange_scratch() * 3 + [
        pltpu.VMEM((CELLS, C), BF),
        pltpu.VMEM((CELLS, C), BF),
        pltpu.VMEM((9, C, C), BF),
        pltpu.VMEM((9, C, C), BF),
        dma((4,)),
        pltpu.VMEM((3, 3 * CP, CP), BF),
        pltpu.VMEM((3, CP, 3 * CP), BF),
        pltpu.VMEM((3, CP, 3 * CP), BF),
        pltpu.VMEM((CELLS, CP), F32),
        pltpu.VMEM((CELLS, CP), F32),
        pltpu.VMEM((CP, CELLS), BF),
        pltpu.VMEM((3, CP, EXT), BF),
        pltpu.VMEM((EXT + 2 * ROW, CP), BF),
        pltpu.VMEM((2, UNITS, 8, 128), BF),
        pltpu.VMEM((CELLS, C), BF),
        dma((1,)),
        pltpu.VMEM((2, UNITS, 8, 128), BF),
    ] + [
        pltpu.VMEM((HALF, 8, 128), BF),
        pltpu.VMEM((HALF, 8, 128), BF),
        pltpu.VMEM((8, 128), F32),
        pltpu.VMEM((3, QUART, 8, 128), BF),
        pltpu.VMEM((QUART, 8, 128), BF),
        pltpu.VMEM((QUART, 8, 128), F32),
        pltpu.VMEM((3, SIXTH, 8, 128), BF),
        pltpu.VMEM((8, SIXTH, 8, 128), BF),
        dma((2,)), dma((2, 3)), dma((2, 3)), dma((2, 7)), dma((2, 3)), dma((2, 3, 4)),
        dma((2, 4)), dma((4,)),
    ] * 2
    dx, ff = pl.pallas_call(
        functools.partial(kernel, n_lon, n_lat),
        out_shape=(jax.ShapeDtypeStruct((CELLS, C), BF),
                   jax.ShapeDtypeStruct((2, UNITS, 8, 128), BF)),
        in_specs=[pl.BlockSpec(memory_space=pltpu.MemorySpace.HBM)] * 4,
        out_specs=(pl.BlockSpec(memory_space=pl.ANY),) * 2,
        scratch_shapes=scratch,
        compiler_params=pltpu.CompilerParams(collective_id=0, has_side_effects=True,
                                             vmem_limit_bytes=32 << 20),
        name="conv_grads",
    )(*(pltpu.with_memory_space_constraint(v, pltpu.MemorySpace.HBM) for v in (
        inputs.reshape(CELLS, C), cotangent.reshape(CELLS, C),
        first_weight.reshape(9, C, C), second_weight.reshape(9, C, C))))
    anywhere = pl.BlockSpec(memory_space=pl.ANY)
    g1, g2, dx = pl.pallas_call(
        functools.partial(finish, scale),
        out_shape=(jax.ShapeDtypeStruct((9 * C, C), F32),) * 2 + (jax.ShapeDtypeStruct((CELLS, C), BF),),
        in_specs=[pl.BlockSpec(memory_space=pltpu.VMEM)] * 2,
        out_specs=(anywhere,) * 3,
        scratch_shapes=[
            pltpu.VMEM((2, 9 * C, C), F32),
            dma((2, 10)),
        ],
        compiler_params=pltpu.CompilerParams(vmem_limit_bytes=24 << 20),
        name="unpack_grads",
    )(ff, dx)
    return (dx.reshape(height, width, channels), g1.reshape(3, 3, C, C), g2.reshape(3, 3, C, C))


def solution(mesh):
    placed = (P("lat", "lon", None), P("lat", "lon", None), P(), P())
    return jax.shard_map(
        functools.partial(shards, mesh.shape["lon"], mesh.shape["lat"]),
        mesh=mesh,
        in_specs=placed,
        out_specs=(P("lat", "lon", None), P(), P()),
        check_vma=False,
    )
```

```python
import functools
import math

import jax
import jax.numpy as jnp
from jax import lax
from jax.experimental import pallas as pl
from jax.experimental.pallas import tpu as pltpu
from jax.sharding import PartitionSpec as P

MESH = pl.DeviceIdType.MESH
BF = jnp.bfloat16
F32 = jnp.float32
ROW = 32
CELLS = 1024
EXT = 1152
C = 192
CP = 256
BLK = 512
UNITS = 352
TAPU = 36


def pack_tail(tail):
    half = tail.shape[0] // 2
    return jnp.concatenate([tail[:half], tail[half:]], axis=1)


def unpack_tail(ref, slot, start, packed):
    n = packed.shape[0]
    zero = jnp.zeros((n, 64), packed.dtype)
    ref[slot, start:start + n, 128:256] = jnp.concatenate([packed[:, :64], zero], axis=1)
    ref[slot, start + n:start + 2 * n, 128:256] = jnp.concatenate([packed[:, 64:], zero], axis=1)


class Exchange:
    def __init__(self, bufs, source, dist, lon, lat, n_lon, n_lat):
        (self.tail, self.rows, self.tail_in, self.rows_in,
         self.send, self.recv, self.ext) = bufs
        self.source = source
        self.lat, self.n_lat = lat, n_lat
        self.lon, self.dist, self.n_lon = lon, dist, n_lon

    def target(self, k):
        if isinstance(k, int) and k == 2:
            return self.lon
        return lax.rem(self.lon + self.n_lon + self.dist * (1 - 2 * k), self.n_lon)

    def crosses(self, k):
        place = lax.rem(self.lon, 16)
        return jnp.where(k == 0, place >= 16 - self.dist, place < self.dist)

    def comes_across(self, k):
        return self.crosses(1 - k)

    def copy(self, src, dst, s, lon, lat):
        return pltpu.make_async_remote_copy(
            src_ref=src, dst_ref=dst, send_sem=self.send.at[s], recv_sem=self.recv.at[s],
            device_id={"lon": lon, "lat": lat}, device_id_type=MESH)

    def main_copy(self, k):
        return self.copy(self.source, self.ext.at[2 * k, pl.ds(ROW, CELLS), pl.ds(0, 128)],
                         k, self.target(k), self.lat)

    def tail_copy(self, k):
        return self.copy(self.tail, self.tail_in.at[k], 2 + k, self.target(k), self.lat)

    def row_copy(self, side):
        lat = jnp.minimum(self.lat + 1, self.n_lat - 1) if side == 0 else jnp.maximum(self.lat - 1, 0)
        return self.copy(self.rows.at[side], self.rows_in.at[4 + side], 4 + side, self.lon, lat)

    def pass_copy(self, k, side):
        return self.copy(self.rows_in.at[4 + side], self.rows_in.at[2 * k + side],
                         6 + 2 * k + side, self.target(k), self.lat)

    def has_row(self, side):
        return self.lat > 0 if side == 0 else self.lat < self.n_lat - 1

    def sends_row(self, side):
        return self.has_row(1 - side)

    def start_slabs(self, across):
        for k in (0, 1):
            @pl.when(self.crosses(k) == across)
            def _():
                self.tail_copy(k).start()
                self.main_copy(k).start()

    def fill_rows(self, last, first):
        for side, part in ((0, last), (1, first)):
            self.rows[side, 0:ROW] = part[:, :128]
            self.rows[side, ROW:] = pack_tail(part[:, 128:C])

    def start_rows(self):
        for side in (0, 1):
            @pl.when(self.sends_row(side))
            def _():
                self.row_copy(side).start()

    def take_rows(self):
        for side in (0, 1):
            @pl.when(self.has_row(side))
            def _():
                self.row_copy(side).wait_recv()

    def pass_rows(self):
        for side in (0, 1):
            @pl.when(self.has_row(side))
            def _():
                for k in (0, 1):
                    self.pass_copy(k, side).start()

    def place_rows(self, k, slot):
        zero = jnp.zeros((ROW, CP), BF)
        for side, start in ((0, 0), (1, ROW + CELLS)):
            @pl.when(self.has_row(side))
            def _():
                packed = self.rows_in[2 * k + side]
                self.ext[slot, start:start + ROW, 0:128] = packed[:ROW]
                unpack_tail(self.ext, slot, start, packed[ROW:])

            @pl.when(jnp.logical_not(self.has_row(side)))
            def _():
                self.ext[slot, start:start + ROW] = zero

    def arrive_rows(self, k):
        for side in (0, 1):
            @pl.when(self.has_row(side))
            def _():
                self.pass_copy(k, side).wait_recv()
        self.place_rows(k, 2 * k)

    def arrive(self, k):
        self.tail_copy(k).wait_recv()
        unpack_tail(self.ext, 2 * k, ROW, self.tail_in[k])
        self.main_copy(k).wait_recv()

    def drain(self):
        for k in (0, 1):
            self.main_copy(k).wait_send()
            self.tail_copy(k).wait_send()
        for side in (0, 1):
            @pl.when(self.sends_row(side))
            def _():
                self.row_copy(side).wait_send()

            @pl.when(self.has_row(side))
            def _():
                for k in (0, 1):
                    self.pass_copy(k, side).wait_send()


def exchange_scratch():
    return [
        pltpu.VMEM((CELLS // 2, 128), BF),
        pltpu.VMEM((2, ROW * 3 // 2, 128), BF),
        pltpu.VMEM((2, CELLS // 2, 128), BF),
        pltpu.VMEM((6, ROW * 3 // 2, 128), BF),
        pltpu.SemaphoreType.DMA((10,)),
        pltpu.SemaphoreType.DMA((10,)),
        pltpu.VMEM((3, EXT, CP), BF),
    ]


HALF, QUART, SIXTH = UNITS // 2, UNITS // 8, UNITS // 32


def remote(src, dst, ss, rs, dev):
    return pltpu.make_async_remote_copy(src_ref=src, dst_ref=dst, send_sem=ss, recv_sem=rs,
                                        device_id=dev, device_id_type=MESH)


class Chain:
    def __init__(self, w, part, ff, out, refs, core, pos1, pos2, z, partner, first, second, third):
        self.w, self.part, self.ff, self.out = w, part, ff, out
        (self.pair_in, self.s0, self.own0, self.r1, self.s1, self.own1, self.r2, self.r3,
         self.pair, self.sem1, self.sem2, self.sem3, self.sem4, self.sem5,
         self.sem6, self.sem7) = refs
        self.core, self.pos1, self.pos2, self.z = core, pos1, pos2, z
        self.partner, self.first, self.second, self.third = partner, first, second, third

    def swap(self):
        return remote(self.part.at[self.w, pl.ds((1 - self.core) * HALF, HALF)], self.pair_in,
                      self.pair.at[0], self.pair.at[1], self.partner)

    def to_first(self, k):
        spot = self.s0.at[pl.ds(lax.rem(self.pos1 + k, 4) * QUART, QUART)]
        return remote(spot, self.r1.at[k - 1], self.sem1.at[0, k - 1], self.sem1.at[1, k - 1], self.first(k))

    def to_second(self, k):
        spot = self.s1.at[pl.ds(lax.rem(self.pos2 + k, 4) * SIXTH, SIXTH)]
        return remote(spot, self.r2.at[k - 1], self.sem2.at[0, k - 1], self.sem2.at[1, k - 1], self.second(k))

    def to_third(self, k, back=0):
        spot = self.r3.at[lax.rem(self.z + back, 8)]
        return remote(spot, spot, self.sem3.at[0, k - 1], self.sem3.at[1, k - 1], self.third(k))

    def place(self, p1, p2, size):
        return self.ff.at[self.w, pl.ds(self.core * HALF + p1 * QUART + p2 * SIXTH, size)]

    def piece(self, k, back=0):
        spot = self.place(self.pos1, lax.rem(self.pos2 + back, 4), SIXTH)
        return remote(spot, spot, self.sem4.at[0, k - 1], self.sem4.at[1, k - 1], self.second(k))

    def spread(self, k, j, back=0):
        spot = self.place(lax.rem(self.pos1 + back, 4), lax.rem(self.pos2 + 4 - j, 4), SIXTH)
        return remote(spot, spot, self.sem5.at[0, k - 1, j], self.sem5.at[1, k - 1, j], self.first(k))

    def back(self, k, theirs=False):
        core = 1 - self.core if theirs else self.core
        spot = pl.ds(core * HALF + lax.rem(self.pos1 + 4 - k, 4) * QUART, QUART)
        return remote(self.ff.at[self.w, spot], self.out.at[self.w, spot],
                      self.sem6.at[0, k], self.sem6.at[1, k], self.partner)

    def keep(self, k):
        spot = pl.ds(self.core * HALF + lax.rem(self.pos1 + 4 - k, 4) * QUART, QUART)
        return pltpu.make_async_copy(self.ff.at[self.w, spot], self.out.at[self.w, spot], self.sem7.at[k])

    def swap_start(self):
        self.swap().start()

    def swap_end(self):
        self.swap().wait()
        mine = self.part[self.w, pl.ds(self.core * HALF, HALF)].astype(F32) + self.pair_in[...].astype(F32)
        self.s0[...] = mine.astype(BF)
        for k in (2, 1, 3):
            self.to_first(k).start()

    def first_end(self):
        spot = pl.ds(self.pos1 * QUART, QUART)
        total = (self.part[self.w, pl.ds(self.core * HALF + self.pos1 * QUART, QUART)].astype(F32)
                 + self.pair_in[spot].astype(F32))
        for k in (1, 2, 3):
            self.to_first(k).wait()
            total += self.r1[k - 1].astype(F32)
        self.own1[...] = total
        self.s1[...] = total.astype(BF)
        for k in (2, 1, 3):
            self.to_second(k).start()

    def second_end(self):
        total = self.own1[pl.ds(self.pos2 * SIXTH, SIXTH)]
        for k in (1, 2, 3):
            self.to_second(k).wait()
            total += self.r2[k - 1].astype(F32)
        self.r3[self.z] = total.astype(BF)
        for k in (4, 3, 5, 2, 6, 1, 7):
            self.to_third(k).start()

    def third_end(self):
        for k in range(1, 8):
            self.to_third(k).wait_send()
            self.to_third(k, 8 - k).wait_recv()
        total = self.r3[0].astype(F32)
        for k in range(1, 8):
            total += self.r3[k].astype(F32)
        self.ff[self.w, pl.ds(self.core * HALF + self.pos1 * QUART + self.pos2 * SIXTH, SIXTH)] = total.astype(BF)
        for k in (2, 1, 3):
            self.piece(k).start()
        for k in (2, 1, 3):
            self.spread(k, 0).start()

    def gather_second(self):
        for j in (1, 3, 2):
            self.piece(j, 4 - j).wait_recv()
            for k in (2, 1, 3):
                self.spread(k, j).start()
        self.back(0).start()
        self.keep(0).start()

    def gather_first(self):
        for k in (1, 3, 2):
            for j in range(4):
                self.spread(k, j, 4 - k).wait_recv()
            self.back(k).start()
            self.keep(k).start()

    def back_end(self):
        for k in range(4):
            self.back(k, True).wait_recv()
            self.keep(k).wait()
        for k in range(4):
            self.back(k).wait_send()
        for k in (1, 2, 3):
            self.piece(k).wait_send()
            for j in range(4):
                self.spread(k, j).wait_send()


def kernel(n_lon, n_lat, x_ref, c_ref, w1_ref, w2_ref, dx_ref, ff_ref, *scratch):
    xb, cb, pb = scratch[0:7], scratch[7:14], scratch[14:21]
    (xv, cv, wv1, wv2, load_sem, w1n, w1t, w2t, acc_x, acc_c, hid_t, x_t, gz, part, dxv, out_sem,
     ff) = scratch[21:38]
    chains = (scratch[38:54], scratch[54:70])
    lon, lat = lax.axis_index("lon"), lax.axis_index("lat")
    core = lax.rem(lon, 2)
    z = lax.rem(lon // 2, 8)
    y = (lon // 16) * 2 + lax.rem(lat, 2)
    x = lat // 2

    def at(xx, yy, zz):
        return {"lon": (yy // 2) * 16 + zz * 2 + core, "lat": xx * 2 + lax.rem(yy, 2)}

    def first(k):
        return at(lax.rem(x + k * (1 - core), 4), lax.rem(y + k * core, 4), z)

    def second(k):
        return at(lax.rem(x + k * core, 4), lax.rem(y + k * (1 - core), 4), z)

    def third(k):
        return at(x, y, lax.rem(z + k, 8))

    partner = {"lon": lon + 1 - 2 * core, "lat": lat}
    pos1 = x * (1 - core) + y * core
    pos2 = y * (1 - core) + x * core

    loads = [pltpu.make_async_copy(src, dst, load_sem.at[i]) for i, (src, dst) in enumerate(
        ((x_ref, xv), (c_ref, cv), (w1_ref, wv1), (w2_ref, wv2)))]
    for load in loads:
        load.start()
    barrier = pltpu.get_barrier_semaphore()

    def greet(dev):
        pl.semaphore_signal(barrier, inc=1, device_id=dev, device_id_type=MESH)

    for dl in (-2, -1, 1, 2):
        greet({"lon": lax.rem(lon + n_lon + dl, n_lon), "lat": lat})
    for da, here in ((-1, lat > 0), (1, lat < n_lat - 1)):
        @pl.when(here)
        def _():
            greet({"lon": lon, "lat": lat + da})
    for k in (1, 2, 3):
        greet(first(k))
        greet(second(k))
    for k in range(1, 8):
        greet(third(k))

    xe = Exchange(xb, x_ref.at[:, pl.ds(0, 128)], 1, lon, lat, n_lon, n_lat)
    ce = Exchange(cb, c_ref.at[:, pl.ds(0, 128)], 2, lon, lat, n_lon, n_lat)
    pe = Exchange(pb, gz.at[pl.ds(2 * ROW, CELLS), pl.ds(0, 128)], 1, lon, lat, n_lon, n_lat)
    for e, v, load in ((xe, xv, loads[0]), (ce, cv, loads[1])):
        load.wait()
        e.fill_rows(v[CELLS - ROW:], v[:ROW])
    beside = jnp.where(lat > 0, 1, 0) + jnp.where(lat < n_lat - 1, 1, 0)
    pl.semaphore_wait(barrier, 4 + 6 + 7 + beside)
    xe.start_rows()
    ce.start_rows()
    xe.tail[...] = pack_tail(xv[:, 128:C])
    xe.start_slabs(False)
    ce.tail[...] = pack_tail(cv[:, 128:C])

    w1n[...] = jnp.zeros_like(w1n)
    w1t[...] = jnp.zeros_like(w1t)
    w2t[...] = jnp.zeros_like(w2t)
    gz[0:2 * ROW] = jnp.zeros((2 * ROW, CP), BF)
    gz[2 * ROW + CELLS:] = jnp.zeros((gz.shape[0] - 2 * ROW - CELLS, CP), BF)
    for e, v in ((xe, xv), (ce, cv)):
        e.ext[1, ROW:ROW + CELLS, 0:128] = v[:, :128]
        e.ext[1, ROW:ROW + CELLS, 128:256] = jnp.concatenate(
            [v[:, 128:C], jnp.zeros((CELLS, 64), BF)], axis=1)
    for w in (0, 1):
        part[w, 324:] = jnp.zeros((UNITS - 324, 8, 128), BF)
    for slot in range(3):
        xe.ext[slot, 2 * ROW + CELLS:] = jnp.zeros((EXT - 2 * ROW - CELLS, CP), BF)
    loads[2].wait()
    loads[3].wait()
    for b in range(3):
        for a in range(3):
            w1n[b, a * CP:a * CP + C, 0:C] = wv1[a * 3 + b]
            w1t[b, 0:C, a * CP:a * CP + C] = wv1[(2 - a) * 3 + 2 - b]
            w2t[b, 0:C, a * CP:a * CP + C] = wv2[(2 - a) * 3 + 2 - b]

    def taps(ext, slot, i):
        start = pl.multiple_of(i * BLK, BLK)
        return jnp.concatenate([ext[slot, pl.ds(start + a * ROW, BLK), :] for a in range(3)], axis=1)

    def straight(ext, slot, i, w):
        return jnp.dot(taps(ext, slot, i), w[slot], preferred_element_type=F32)

    def flipped(ext, slot, i, w):
        return lax.dot_general(taps(ext, slot, i), w[slot], (((1,), (1,)), ((), ())),
                               preferred_element_type=F32)

    def rows_of(i):
        return pl.ds(pl.multiple_of(i * BLK, BLK), BLK)

    def add_slab(acc, conv, ext, slot, w, new):
        @pl.loop(0, CELLS // BLK)
        def _(i):
            value = conv(ext, slot, i, w)
            acc[rows_of(i)] = value if new else acc[rows_of(i)] + value

    def put_tap(which, tap, grad):
        main = grad[:, :128].reshape(24, 8, 128)
        tail = jnp.concatenate([grad[:96, 128:C], grad[96:, 128:C]], axis=1).reshape(12, 8, 128)
        part[which, pl.ds(tap * TAPU, 24)] = main.astype(BF)
        part[which, pl.ds(tap * TAPU + 24, 12)] = tail.astype(BF)

    xe.take_rows()
    ce.take_rows()
    xe.start_slabs(True)
    xe.pass_rows()
    ce.pass_rows()
    ce.start_slabs(False)
    ce.start_slabs(True)
    xe.place_rows(2, 1)
    ce.place_rows(2, 1)
    add_slab(acc_x, straight, xe.ext, 1, w1n, True)
    x_t[1] = xe.ext[1].T

    def take_x(k):
        xe.arrive_rows(k)
        xe.arrive(k)
        add_slab(acc_x, straight, xe.ext, 2 * k, w1n, False)
        x_t[2 * k] = xe.ext[2 * k].T

    take_x(1 - core)
    add_slab(acc_c, flipped, ce.ext, 1, w2t, True)
    take_x(core)

    @pl.loop(0, CELLS // BLK)
    def _(i):
        pre = acc_x[rows_of(i)]
        sig = 1.0 / (1.0 + jnp.exp(-pre))
        hid_t[:, rows_of(i)] = (pre * sig).astype(BF).T
        acc_x[rows_of(i)] = sig * (1.0 + pre * (1.0 - sig))

    def second_grad(slot):
        @pl.loop(0, 3)
        def _(a):
            rhs = ce.ext[slot, pl.ds(pl.multiple_of((2 - a) * ROW, ROW), CELLS), :]
            put_tap(1, a * 3 + 2 - slot, jnp.dot(hid_t[0:C], rhs, preferred_element_type=F32))

    second_grad(1)
    late = jnp.where(ce.comes_across(0), 0, 1)
    for k in (1 - late, late):
        ce.arrive_rows(k)
        ce.arrive(k)
        add_slab(acc_c, flipped, ce.ext, 2 * k, w2t, False)

    @pl.loop(0, CELLS // BLK)
    def _(i):
        value = (acc_c[rows_of(i)] * acc_x[rows_of(i)]).astype(BF)
        gz[pl.ds(pl.multiple_of(i * BLK + 2 * ROW, 2 * ROW), BLK)] = value
        pe.ext[1, pl.ds(pl.multiple_of(i * BLK + ROW, ROW), BLK)] = value
    pe.fill_rows(gz[CELLS + ROW:CELLS + 2 * ROW], gz[2 * ROW:3 * ROW])
    pe.start_rows()
    pe.tail[...] = pack_tail(gz[2 * ROW:2 * ROW + CELLS, 128:C])
    pe.start_slabs(True)
    pe.start_slabs(False)

    @pl.loop(0, 3)
    def _(a):
        rhs = gz[pl.ds(pl.multiple_of((2 - a) * ROW, ROW), EXT), :]
        for b in range(3):
            put_tap(0, a * 3 + b, jnp.dot(x_t[b, 0:C], rhs, preferred_element_type=F32))

    one, two = (Chain(w, part, ff, ff_ref, refs, core, pos1, pos2, z, partner, first, second, third)
                for w, refs in enumerate(chains))
    one.swap_start()
    second_grad(0)
    second_grad(2)
    two.swap_start()
    one.swap_end()
    pe.take_rows()
    pe.pass_rows()
    pe.place_rows(2, 1)
    add_slab(acc_x, flipped, pe.ext, 1, w1t, True)
    two.swap_end()

    def take_p(k):
        pe.arrive_rows(k)
        pe.arrive(k)
        add_slab(acc_x, flipped, pe.ext, 2 * k, w1t, False)

    take_p(1 - core)
    one.first_end()
    take_p(core)
    two.first_end()
    one.second_end()
    two.second_end()
    xe.drain()
    ce.drain()
    one.third_end()
    two.third_end()
    one.gather_second()
    two.gather_second()
    one.gather_first()
    two.gather_first()

    @pl.loop(0, CELLS // BLK)
    def _(i):
        dxv[rows_of(i)] = acc_x[rows_of(i), 0:C].astype(BF)
    dx_out = pltpu.make_async_copy(dxv, dx_ref, out_sem.at[0])
    dx_out.start()
    pe.drain()
    for chain in (one, two):
        chain.back_end()
    dx_out.wait()


def finish(scale, ffv, dxv, g1_ref, g2_ref, out_ref, gv, sem_out):
    taps = [(t, which) for t in (0, 3, 6) for which in (0, 1)]

    def give(t, which):
        rows = pl.ds(t * C, 3 * C)
        return pltpu.make_async_copy(gv.at[which, rows], (g1_ref, g2_ref)[which].at[rows], sem_out.at[which, t])

    dx_out = pltpu.make_async_copy(dxv, out_ref, sem_out.at[0, 9])
    dx_out.start()
    for t, which in taps:
        for u in range(t, t + 3):
            main = ffv[which, u * TAPU:u * TAPU + 24].astype(F32).reshape(C, 128) * scale
            tail = ffv[which, u * TAPU + 24:(u + 1) * TAPU].astype(F32).reshape(96, 128) * scale
            row = u * C
            gv[which, row:row + C, 0:128] = main
            gv[which, row:row + 96, 128:C] = tail[:, :64]
            gv[which, row + 96:row + C, 128:C] = tail[:, 64:]
        give(t, which).start()
    for tap in taps:
        give(*tap).wait()
    dx_out.wait()


def shards(n_lon, n_lat, inputs, cotangent, first_weight, second_weight):
    height, width, channels = inputs.shape
    scale = 1.0 / math.sqrt(height * n_lat * width * n_lon)
    dma = pltpu.SemaphoreType.DMA
    scratch = exchange_scratch() * 3 + [
        pltpu.VMEM((CELLS, C), BF),
        pltpu.VMEM((CELLS, C), BF),
        pltpu.VMEM((9, C, C), BF),
        pltpu.VMEM((9, C, C), BF),
        dma((4,)),
        pltpu.VMEM((3, 3 * CP, CP), BF),
        pltpu.VMEM((3, CP, 3 * CP), BF),
        pltpu.VMEM((3, CP, 3 * CP), BF),
        pltpu.VMEM((CELLS, CP), F32),
        pltpu.VMEM((CELLS, CP), F32),
        pltpu.VMEM((CP, CELLS), BF),
        pltpu.VMEM((3, CP, EXT), BF),
        pltpu.VMEM((EXT + 2 * ROW, CP), BF),
        pltpu.VMEM((2, UNITS, 8, 128), BF),
        pltpu.VMEM((CELLS, C), BF),
        dma((1,)),
        pltpu.VMEM((2, UNITS, 8, 128), BF),
    ] + [
        pltpu.VMEM((HALF, 8, 128), BF),
        pltpu.VMEM((HALF, 8, 128), BF),
        pltpu.VMEM((8, 128), F32),
        pltpu.VMEM((3, QUART, 8, 128), BF),
        pltpu.VMEM((QUART, 8, 128), BF),
        pltpu.VMEM((QUART, 8, 128), F32),
        pltpu.VMEM((3, SIXTH, 8, 128), BF),
        pltpu.VMEM((8, SIXTH, 8, 128), BF),
        dma((2,)), dma((2, 3)), dma((2, 3)), dma((2, 7)), dma((2, 3)), dma((2, 3, 4)),
        dma((2, 4)), dma((4,)),
    ] * 2
    dx, ff = pl.pallas_call(
        functools.partial(kernel, n_lon, n_lat),
        out_shape=(jax.ShapeDtypeStruct((CELLS, C), BF),
                   jax.ShapeDtypeStruct((2, UNITS, 8, 128), BF)),
        in_specs=[pl.BlockSpec(memory_space=pltpu.MemorySpace.HBM)] * 4,
        out_specs=(pl.BlockSpec(memory_space=pl.ANY),) * 2,
        scratch_shapes=scratch,
        compiler_params=pltpu.CompilerParams(collective_id=0, has_side_effects=True,
                                             vmem_limit_bytes=32 << 20),
        name="conv_grads",
    )(*(pltpu.with_memory_space_constraint(v, pltpu.MemorySpace.HBM) for v in (
        inputs.reshape(CELLS, C), cotangent.reshape(CELLS, C),
        first_weight.reshape(9, C, C), second_weight.reshape(9, C, C))))
    anywhere = pl.BlockSpec(memory_space=pl.ANY)
    g1, g2, dx = pl.pallas_call(
        functools.partial(finish, scale),
        out_shape=(jax.ShapeDtypeStruct((9 * C, C), F32),) * 2 + (jax.ShapeDtypeStruct((CELLS, C), BF),),
        in_specs=[pl.BlockSpec(memory_space=pltpu.VMEM)] * 2,
        out_specs=(anywhere,) * 3,
        scratch_shapes=[
            pltpu.VMEM((2, 9 * C, C), F32),
            dma((2, 10)),
        ],
        compiler_params=pltpu.CompilerParams(vmem_limit_bytes=24 << 20),
        name="unpack_grads",
    )(ff, dx)
    return (dx.reshape(height, width, channels), g1.reshape(3, 3, C, C), g2.reshape(3, 3, C, C))


def solution(mesh):
    placed = (P("lat", "lon", None), P("lat", "lon", None), P(), P())
    return jax.shard_map(
        functools.partial(shards, mesh.shape["lon"], mesh.shape["lat"]),
        mesh=mesh,
        in_specs=placed,
        out_specs=(P("lat", "lon", None), P(), P()),
        check_vma=False,
    )
```

```python
import functools
import math

import jax
import jax.numpy as jnp
from jax import lax
from jax.experimental import pallas as pl
from jax.experimental.pallas import tpu as pltpu
from jax.sharding import PartitionSpec as P

MESH = pl.DeviceIdType.MESH
BF = jnp.bfloat16
F32 = jnp.float32
ROW = 32
CELLS = 1024
EXT = 1152
C = 192
CP = 256
BLK = 512
UNITS = 352
TAPU = 36


def pack_tail(tail):
    half = tail.shape[0] // 2
    return jnp.concatenate([tail[:half], tail[half:]], axis=1)


def unpack_tail(ref, slot, start, packed):
    n = packed.shape[0]
    zero = jnp.zeros((n, 64), packed.dtype)
    ref[slot, start:start + n, 128:256] = jnp.concatenate([packed[:, :64], zero], axis=1)
    ref[slot, start + n:start + 2 * n, 128:256] = jnp.concatenate([packed[:, 64:], zero], axis=1)


class Exchange:
    def __init__(self, bufs, source, dist, lon, lat, n_lon, n_lat):
        (self.tail, self.rows, self.tail_in, self.rows_in,
         self.send, self.recv, self.ext) = bufs
        self.source = source
        self.lat, self.n_lat = lat, n_lat
        self.lon, self.dist, self.n_lon = lon, dist, n_lon

    def target(self, k):
        if isinstance(k, int) and k == 2:
            return self.lon
        return lax.rem(self.lon + self.n_lon + self.dist * (1 - 2 * k), self.n_lon)

    def crosses(self, k):
        place = lax.rem(self.lon, 16)
        return jnp.where(k == 0, place >= 16 - self.dist, place < self.dist)

    def comes_across(self, k):
        return self.crosses(1 - k)

    def copy(self, src, dst, s, lon, lat):
        return pltpu.make_async_remote_copy(
            src_ref=src, dst_ref=dst, send_sem=self.send.at[s], recv_sem=self.recv.at[s],
            device_id={"lon": lon, "lat": lat}, device_id_type=MESH)

    def main_copy(self, k):
        return self.copy(self.source, self.ext.at[2 * k, pl.ds(ROW, CELLS), pl.ds(0, 128)],
                         k, self.target(k), self.lat)

    def tail_copy(self, k):
        return self.copy(self.tail, self.tail_in.at[k], 2 + k, self.target(k), self.lat)

    def row_copy(self, side):
        lat = jnp.minimum(self.lat + 1, self.n_lat - 1) if side == 0 else jnp.maximum(self.lat - 1, 0)
        return self.copy(self.rows.at[side], self.rows_in.at[4 + side], 4 + side, self.lon, lat)

    def pass_copy(self, k, side):
        return self.copy(self.rows_in.at[4 + side], self.rows_in.at[2 * k + side],
                         6 + 2 * k + side, self.target(k), self.lat)

    def has_row(self, side):
        return self.lat > 0 if side == 0 else self.lat < self.n_lat - 1

    def sends_row(self, side):
        return self.has_row(1 - side)

    def start_slabs(self, across, ks=(0, 1)):
        for k in ks:
            @pl.when(self.crosses(k) == across)
            def _():
                self.tail_copy(k).start()
                self.main_copy(k).start()

    def fill_rows(self, last, first):
        for side, part in ((0, last), (1, first)):
            self.rows[side, 0:ROW] = part[:, :128]
            self.rows[side, ROW:] = pack_tail(part[:, 128:C])

    def start_rows(self):
        for side in (0, 1):
            @pl.when(self.sends_row(side))
            def _():
                self.row_copy(side).start()

    def take_rows(self):
        for side in (0, 1):
            @pl.when(self.has_row(side))
            def _():
                self.row_copy(side).wait_recv()

    def pass_rows(self):
        for side in (0, 1):
            @pl.when(self.has_row(side))
            def _():
                for k in (0, 1):
                    self.pass_copy(k, side).start()

    def place_rows(self, k, slot):
        zero = jnp.zeros((ROW, CP), BF)
        for side, start in ((0, 0), (1, ROW + CELLS)):
            @pl.when(self.has_row(side))
            def _():
                packed = self.rows_in[2 * k + side]
                self.ext[slot, start:start + ROW, 0:128] = packed[:ROW]
                unpack_tail(self.ext, slot, start, packed[ROW:])

            @pl.when(jnp.logical_not(self.has_row(side)))
            def _():
                self.ext[slot, start:start + ROW] = zero

    def arrive_rows(self, k):
        for side in (0, 1):
            @pl.when(self.has_row(side))
            def _():
                self.pass_copy(k, side).wait_recv()
        self.place_rows(k, 2 * k)

    def arrive(self, k):
        self.tail_copy(k).wait_recv()
        unpack_tail(self.ext, 2 * k, ROW, self.tail_in[k])
        self.main_copy(k).wait_recv()

    def drain(self):
        for k in (0, 1):
            self.main_copy(k).wait_send()
            self.tail_copy(k).wait_send()
        for side in (0, 1):
            @pl.when(self.sends_row(side))
            def _():
                self.row_copy(side).wait_send()

            @pl.when(self.has_row(side))
            def _():
                for k in (0, 1):
                    self.pass_copy(k, side).wait_send()


def exchange_scratch():
    return [
        pltpu.VMEM((CELLS // 2, 128), BF),
        pltpu.VMEM((2, ROW * 3 // 2, 128), BF),
        pltpu.VMEM((2, CELLS // 2, 128), BF),
        pltpu.VMEM((6, ROW * 3 // 2, 128), BF),
        pltpu.SemaphoreType.DMA((10,)),
        pltpu.SemaphoreType.DMA((10,)),
        pltpu.VMEM((3, EXT, CP), BF),
    ]


HALF, QUART, SIXTH = UNITS // 2, UNITS // 8, UNITS // 32


def remote(src, dst, ss, rs, dev):
    return pltpu.make_async_remote_copy(src_ref=src, dst_ref=dst, send_sem=ss, recv_sem=rs,
                                        device_id=dev, device_id_type=MESH)


class Chain:
    def __init__(self, w, part, ff, out, refs, core, pos1, pos2, z, partner, first, second, third):
        self.w, self.part, self.ff, self.out = w, part, ff, out
        (self.pair_in, self.s0, self.own0, self.r1, self.s1, self.own1, self.r2, self.r3,
         self.pair, self.sem1, self.sem2, self.sem3, self.sem4, self.sem5,
         self.sem6, self.sem7) = refs
        self.core, self.pos1, self.pos2, self.z = core, pos1, pos2, z
        self.partner, self.first, self.second, self.third = partner, first, second, third

    def swap(self):
        return remote(self.part.at[self.w, pl.ds((1 - self.core) * HALF, HALF)], self.pair_in,
                      self.pair.at[0], self.pair.at[1], self.partner)

    def to_first(self, k):
        spot = self.s0.at[pl.ds(lax.rem(self.pos1 + k, 4) * QUART, QUART)]
        return remote(spot, self.r1.at[k - 1], self.sem1.at[0, k - 1], self.sem1.at[1, k - 1], self.first(k))

    def to_second(self, k):
        spot = self.s1.at[pl.ds(lax.rem(self.pos2 + k, 4) * SIXTH, SIXTH)]
        return remote(spot, self.r2.at[k - 1], self.sem2.at[0, k - 1], self.sem2.at[1, k - 1], self.second(k))

    def to_third(self, k, back=0):
        spot = self.r3.at[lax.rem(self.z + back, 8)]
        return remote(spot, spot, self.sem3.at[0, k - 1], self.sem3.at[1, k - 1], self.third(k))

    def place(self, p1, p2, size):
        return self.ff.at[self.w, pl.ds(self.core * HALF + p1 * QUART + p2 * SIXTH, size)]

    def piece(self, k, back=0):
        spot = self.place(self.pos1, lax.rem(self.pos2 + back, 4), SIXTH)
        return remote(spot, spot, self.sem4.at[0, k - 1], self.sem4.at[1, k - 1], self.second(k))

    def spread(self, k, j, back=0):
        spot = self.place(lax.rem(self.pos1 + back, 4), lax.rem(self.pos2 + 4 - j, 4), SIXTH)
        return remote(spot, spot, self.sem5.at[0, k - 1, j], self.sem5.at[1, k - 1, j], self.first(k))

    def back(self, k, theirs=False):
        core = 1 - self.core if theirs else self.core
        spot = pl.ds(core * HALF + lax.rem(self.pos1 + 4 - k, 4) * QUART, QUART)
        return remote(self.ff.at[self.w, spot], self.out.at[self.w, spot],
                      self.sem6.at[0, k], self.sem6.at[1, k], self.partner)

    def keep(self, k):
        spot = pl.ds(self.core * HALF + lax.rem(self.pos1 + 4 - k, 4) * QUART, QUART)
        return pltpu.make_async_copy(self.ff.at[self.w, spot], self.out.at[self.w, spot], self.sem7.at[k])

    def swap_start(self):
        self.swap().start()

    def swap_end(self):
        self.swap().wait()
        mine = self.part[self.w, pl.ds(self.core * HALF, HALF)].astype(F32) + self.pair_in[...].astype(F32)
        self.s0[...] = mine.astype(BF)
        for k in (2, 1, 3):
            self.to_first(k).start()

    def first_end(self):
        spot = pl.ds(self.pos1 * QUART, QUART)
        total = (self.part[self.w, pl.ds(self.core * HALF + self.pos1 * QUART, QUART)].astype(F32)
                 + self.pair_in[spot].astype(F32))
        for k in (1, 2, 3):
            self.to_first(k).wait()
            total += self.r1[k - 1].astype(F32)
        self.own1[...] = total
        self.s1[...] = total.astype(BF)
        for k in (2, 1, 3):
            self.to_second(k).start()

    def second_end(self):
        total = self.own1[pl.ds(self.pos2 * SIXTH, SIXTH)]
        for k in (1, 2, 3):
            self.to_second(k).wait()
            total += self.r2[k - 1].astype(F32)
        self.r3[self.z] = total.astype(BF)
        for k in (4, 3, 5, 2, 6, 1, 7):
            self.to_third(k).start()

    def third_end(self):
        for k in range(1, 8):
            self.to_third(k).wait_send()
            self.to_third(k, 8 - k).wait_recv()
        total = self.r3[0].astype(F32)
        for k in range(1, 8):
            total += self.r3[k].astype(F32)
        self.ff[self.w, pl.ds(self.core * HALF + self.pos1 * QUART + self.pos2 * SIXTH, SIXTH)] = total.astype(BF)
        for k in (2, 1, 3):
            self.piece(k).start()
        for k in (2, 1, 3):
            self.spread(k, 0).start()

    def gather_second(self):
        for j in (1, 3, 2):
            self.piece(j, 4 - j).wait_recv()
            for k in (2, 1, 3):
                self.spread(k, j).start()
        self.back(0).start()
        self.keep(0).start()

    def gather_first(self):
        for k in (1, 3, 2):
            for j in range(4):
                self.spread(k, j, 4 - k).wait_recv()
            self.back(k).start()
            self.keep(k).start()

    def back_end(self):
        for k in range(4):
            self.back(k, True).wait_recv()
            self.keep(k).wait()
        for k in range(4):
            self.back(k).wait_send()
        for k in (1, 2, 3):
            self.piece(k).wait_send()
            for j in range(4):
                self.spread(k, j).wait_send()


def kernel(n_lon, n_lat, x_ref, c_ref, w1_ref, w2_ref, dx_ref, ff_ref, *scratch):
    xb, cb, pb = scratch[0:7], scratch[7:14], scratch[14:21]
    (xv, cv, wv1, wv2, load_sem, w1n, w1t, w2t, acc_x, acc_c, hid_t, x_t, gz, part, dxv, out_sem,
     ff) = scratch[21:38]
    chains = (scratch[38:54], scratch[54:70])
    lon, lat = lax.axis_index("lon"), lax.axis_index("lat")
    core = lax.rem(lon, 2)
    z = lax.rem(lon // 2, 8)
    y = (lon // 16) * 2 + lax.rem(lat, 2)
    x = lat // 2

    def at(xx, yy, zz):
        return {"lon": (yy // 2) * 16 + zz * 2 + core, "lat": xx * 2 + lax.rem(yy, 2)}

    def first(k):
        return at(lax.rem(x + k * (1 - core), 4), lax.rem(y + k * core, 4), z)

    def second(k):
        return at(lax.rem(x + k * core, 4), lax.rem(y + k * (1 - core), 4), z)

    def third(k):
        return at(x, y, lax.rem(z + k, 8))

    partner = {"lon": lon + 1 - 2 * core, "lat": lat}
    pos1 = x * (1 - core) + y * core
    pos2 = y * (1 - core) + x * core

    loads = [pltpu.make_async_copy(src, dst, load_sem.at[i]) for i, (src, dst) in enumerate(
        ((x_ref, xv), (c_ref, cv), (w1_ref, wv1), (w2_ref, wv2)))]
    for load in loads:
        load.start()
    barrier = pltpu.get_barrier_semaphore()

    def greet(dev):
        pl.semaphore_signal(barrier, inc=1, device_id=dev, device_id_type=MESH)

    for dl in (-2, -1, 1, 2):
        greet({"lon": lax.rem(lon + n_lon + dl, n_lon), "lat": lat})
    for da, here in ((-1, lat > 0), (1, lat < n_lat - 1)):
        @pl.when(here)
        def _():
            greet({"lon": lon, "lat": lat + da})
    for k in (1, 2, 3):
        greet(first(k))
        greet(second(k))
    for k in range(1, 8):
        greet(third(k))

    xe = Exchange(xb, x_ref.at[:, pl.ds(0, 128)], 1, lon, lat, n_lon, n_lat)
    ce = Exchange(cb, c_ref.at[:, pl.ds(0, 128)], 2, lon, lat, n_lon, n_lat)
    pe = Exchange(pb, gz.at[pl.ds(2 * ROW, CELLS), pl.ds(0, 128)], 1, lon, lat, n_lon, n_lat)
    for e, v, load in ((xe, xv, loads[0]), (ce, cv, loads[1])):
        load.wait()
        e.fill_rows(v[CELLS - ROW:], v[:ROW])
    beside = jnp.where(lat > 0, 1, 0) + jnp.where(lat < n_lat - 1, 1, 0)
    pl.semaphore_wait(barrier, 4 + 6 + 7 + beside)
    xe.start_rows()
    ce.start_rows()
    xe.tail[...] = pack_tail(xv[:, 128:C])
    xe.start_slabs(False)
    xe.start_slabs(True, (1,))
    ce.tail[...] = pack_tail(cv[:, 128:C])

    w1n[...] = jnp.zeros_like(w1n)
    w1t[...] = jnp.zeros_like(w1t)
    w2t[...] = jnp.zeros_like(w2t)
    gz[0:2 * ROW] = jnp.zeros((2 * ROW, CP), BF)
    gz[2 * ROW + CELLS:] = jnp.zeros((gz.shape[0] - 2 * ROW - CELLS, CP), BF)
    for e, v in ((xe, xv), (ce, cv)):
        e.ext[1, ROW:ROW + CELLS, 0:128] = v[:, :128]
        e.ext[1, ROW:ROW + CELLS, 128:256] = jnp.concatenate(
            [v[:, 128:C], jnp.zeros((CELLS, 64), BF)], axis=1)
    for w in (0, 1):
        part[w, 324:] = jnp.zeros((UNITS - 324, 8, 128), BF)
    for slot in range(3):
        xe.ext[slot, 2 * ROW + CELLS:] = jnp.zeros((EXT - 2 * ROW - CELLS, CP), BF)
    loads[2].wait()
    loads[3].wait()
    for b in range(3):
        for a in range(3):
            w1n[b, a * CP:a * CP + C, 0:C] = wv1[a * 3 + b]
            w1t[b, 0:C, a * CP:a * CP + C] = wv1[(2 - a) * 3 + 2 - b]
            w2t[b, 0:C, a * CP:a * CP + C] = wv2[(2 - a) * 3 + 2 - b]

    def taps(ext, slot, i):
        start = pl.multiple_of(i * BLK, BLK)
        return jnp.concatenate([ext[slot, pl.ds(start + a * ROW, BLK), :] for a in range(3)], axis=1)

    def straight(ext, slot, i, w):
        return jnp.dot(taps(ext, slot, i), w[slot], preferred_element_type=F32)

    def flipped(ext, slot, i, w):
        return lax.dot_general(taps(ext, slot, i), w[slot], (((1,), (1,)), ((), ())),
                               preferred_element_type=F32)

    def rows_of(i):
        return pl.ds(pl.multiple_of(i * BLK, BLK), BLK)

    def add_slab(acc, conv, ext, slot, w, new):
        @pl.loop(0, CELLS // BLK)
        def _(i):
            value = conv(ext, slot, i, w)
            acc[rows_of(i)] = value if new else acc[rows_of(i)] + value

    def put_tap(which, tap, grad):
        main = grad[:, :128].reshape(24, 8, 128)
        tail = jnp.concatenate([grad[:96, 128:C], grad[96:, 128:C]], axis=1).reshape(12, 8, 128)
        part[which, pl.ds(tap * TAPU, 24)] = main.astype(BF)
        part[which, pl.ds(tap * TAPU + 24, 12)] = tail.astype(BF)

    xe.take_rows()
    ce.take_rows()
    xe.start_slabs(True, (0,))
    xe.pass_rows()
    ce.pass_rows()
    ce.start_slabs(False)
    ce.start_slabs(True)
    xe.place_rows(2, 1)
    ce.place_rows(2, 1)
    add_slab(acc_x, straight, xe.ext, 1, w1n, True)
    x_t[1] = xe.ext[1].T

    def take_x(k):
        xe.arrive_rows(k)
        xe.arrive(k)
        add_slab(acc_x, straight, xe.ext, 2 * k, w1n, False)
        x_t[2 * k] = xe.ext[2 * k].T

    take_x(1 - core)
    add_slab(acc_c, flipped, ce.ext, 1, w2t, True)
    take_x(core)

    @pl.loop(0, CELLS // BLK)
    def _(i):
        pre = acc_x[rows_of(i)]
        sig = 1.0 / (1.0 + jnp.exp(-pre))
        hid_t[:, rows_of(i)] = (pre * sig).astype(BF).T
        acc_x[rows_of(i)] = sig * (1.0 + pre * (1.0 - sig))

    def second_grad(slot):
        @pl.loop(0, 3)
        def _(a):
            rhs = ce.ext[slot, pl.ds(pl.multiple_of((2 - a) * ROW, ROW), CELLS), :]
            put_tap(1, a * 3 + 2 - slot, jnp.dot(hid_t[0:C], rhs, preferred_element_type=F32))

    second_grad(1)
    late = jnp.where(ce.comes_across(0), 0, 1)
    for k in (1 - late, late):
        ce.arrive_rows(k)
        ce.arrive(k)
        add_slab(acc_c, flipped, ce.ext, 2 * k, w2t, False)

    @pl.loop(0, CELLS // BLK)
    def _(i):
        value = (acc_c[rows_of(i)] * acc_x[rows_of(i)]).astype(BF)
        gz[pl.ds(pl.multiple_of(i * BLK + 2 * ROW, 2 * ROW), BLK)] = value
        pe.ext[1, pl.ds(pl.multiple_of(i * BLK + ROW, ROW), BLK)] = value
    pe.fill_rows(gz[CELLS + ROW:CELLS + 2 * ROW], gz[2 * ROW:3 * ROW])
    pe.start_rows()
    pe.tail[...] = pack_tail(gz[2 * ROW:2 * ROW + CELLS, 128:C])
    pe.start_slabs(True)
    pe.start_slabs(False)

    @pl.loop(0, 3)
    def _(a):
        rhs = gz[pl.ds(pl.multiple_of((2 - a) * ROW, ROW), EXT), :]
        for b in range(3):
            put_tap(0, a * 3 + b, jnp.dot(x_t[b, 0:C], rhs, preferred_element_type=F32))

    one, two = (Chain(w, part, ff, ff_ref, refs, core, pos1, pos2, z, partner, first, second, third)
                for w, refs in enumerate(chains))
    one.swap_start()
    second_grad(0)
    second_grad(2)
    two.swap_start()
    one.swap_end()
    two.swap_end()
    pe.take_rows()
    pe.pass_rows()
    pe.place_rows(2, 1)
    add_slab(acc_x, flipped, pe.ext, 1, w1t, True)

    def take_p(k):
        pe.arrive_rows(k)
        pe.arrive(k)
        add_slab(acc_x, flipped, pe.ext, 2 * k, w1t, False)

    take_p(1 - core)
    one.first_end()
    take_p(core)
    two.first_end()
    one.second_end()
    two.second_end()
    xe.drain()
    ce.drain()
    one.third_end()
    two.third_end()
    one.gather_second()
    two.gather_second()
    one.gather_first()
    two.gather_first()

    @pl.loop(0, CELLS // BLK)
    def _(i):
        dxv[rows_of(i)] = acc_x[rows_of(i), 0:C].astype(BF)
    dx_out = pltpu.make_async_copy(dxv, dx_ref, out_sem.at[0])
    dx_out.start()
    pe.drain()
    for chain in (one, two):
        chain.back_end()
    dx_out.wait()


def finish(scale, ffv, dxv, g1_ref, g2_ref, out_ref, gv, sem_out):
    taps = [(t, which) for t in (0, 3, 6) for which in (0, 1)]

    def give(t, which):
        rows = pl.ds(t * C, 3 * C)
        return pltpu.make_async_copy(gv.at[which, rows], (g1_ref, g2_ref)[which].at[rows], sem_out.at[which, t])

    dx_out = pltpu.make_async_copy(dxv, out_ref, sem_out.at[0, 9])
    dx_out.start()
    for t, which in taps:
        for u in range(t, t + 3):
            main = ffv[which, u * TAPU:u * TAPU + 24].astype(F32).reshape(C, 128) * scale
            tail = ffv[which, u * TAPU + 24:(u + 1) * TAPU].astype(F32).reshape(96, 128) * scale
            row = u * C
            gv[which, row:row + C, 0:128] = main
            gv[which, row:row + 96, 128:C] = tail[:, :64]
            gv[which, row + 96:row + C, 128:C] = tail[:, 64:]
        give(t, which).start()
    for tap in taps:
        give(*tap).wait()
    dx_out.wait()


def shards(n_lon, n_lat, inputs, cotangent, first_weight, second_weight):
    height, width, channels = inputs.shape
    scale = 1.0 / math.sqrt(height * n_lat * width * n_lon)
    dma = pltpu.SemaphoreType.DMA
    scratch = exchange_scratch() * 3 + [
        pltpu.VMEM((CELLS, C), BF),
        pltpu.VMEM((CELLS, C), BF),
        pltpu.VMEM((9, C, C), BF),
        pltpu.VMEM((9, C, C), BF),
        dma((4,)),
        pltpu.VMEM((3, 3 * CP, CP), BF),
        pltpu.VMEM((3, CP, 3 * CP), BF),
        pltpu.VMEM((3, CP, 3 * CP), BF),
        pltpu.VMEM((CELLS, CP), F32),
        pltpu.VMEM((CELLS, CP), F32),
        pltpu.VMEM((CP, CELLS), BF),
        pltpu.VMEM((3, CP, EXT), BF),
        pltpu.VMEM((EXT + 2 * ROW, CP), BF),
        pltpu.VMEM((2, UNITS, 8, 128), BF),
        pltpu.VMEM((CELLS, C), BF),
        dma((1,)),
        pltpu.VMEM((2, UNITS, 8, 128), BF),
    ] + [
        pltpu.VMEM((HALF, 8, 128), BF),
        pltpu.VMEM((HALF, 8, 128), BF),
        pltpu.VMEM((8, 128), F32),
        pltpu.VMEM((3, QUART, 8, 128), BF),
        pltpu.VMEM((QUART, 8, 128), BF),
        pltpu.VMEM((QUART, 8, 128), F32),
        pltpu.VMEM((3, SIXTH, 8, 128), BF),
        pltpu.VMEM((8, SIXTH, 8, 128), BF),
        dma((2,)), dma((2, 3)), dma((2, 3)), dma((2, 7)), dma((2, 3)), dma((2, 3, 4)),
        dma((2, 4)), dma((4,)),
    ] * 2
    dx, ff = pl.pallas_call(
        functools.partial(kernel, n_lon, n_lat),
        out_shape=(jax.ShapeDtypeStruct((CELLS, C), BF),
                   jax.ShapeDtypeStruct((2, UNITS, 8, 128), BF)),
        in_specs=[pl.BlockSpec(memory_space=pltpu.MemorySpace.HBM)] * 4,
        out_specs=(pl.BlockSpec(memory_space=pl.ANY),) * 2,
        scratch_shapes=scratch,
        compiler_params=pltpu.CompilerParams(collective_id=0, has_side_effects=True,
                                             vmem_limit_bytes=32 << 20),
        name="conv_grads",
    )(*(pltpu.with_memory_space_constraint(v, pltpu.MemorySpace.HBM) for v in (
        inputs.reshape(CELLS, C), cotangent.reshape(CELLS, C),
        first_weight.reshape(9, C, C), second_weight.reshape(9, C, C))))
    anywhere = pl.BlockSpec(memory_space=pl.ANY)
    g1, g2, dx = pl.pallas_call(
        functools.partial(finish, scale),
        out_shape=(jax.ShapeDtypeStruct((9 * C, C), F32),) * 2 + (jax.ShapeDtypeStruct((CELLS, C), BF),),
        in_specs=[pl.BlockSpec(memory_space=pltpu.VMEM)] * 2,
        out_specs=(anywhere,) * 3,
        scratch_shapes=[
            pltpu.VMEM((2, 9 * C, C), F32),
            dma((2, 10)),
        ],
        compiler_params=pltpu.CompilerParams(vmem_limit_bytes=24 << 20),
        name="unpack_grads",
    )(ff, dx)
    return (dx.reshape(height, width, channels), g1.reshape(3, 3, C, C), g2.reshape(3, 3, C, C))


def solution(mesh):
    placed = (P("lat", "lon", None), P("lat", "lon", None), P(), P())
    return jax.shard_map(
        functools.partial(shards, mesh.shape["lon"], mesh.shape["lat"]),
        mesh=mesh,
        in_specs=placed,
        out_specs=(P("lat", "lon", None), P(), P()),
        check_vma=False,
    )
```
